512 devices in a mesh: dp: 64 (over z_hi, y, core), rows: 8 (over z_lo, x).
Axes of the slice: x: 4, y: 8, z: 8 (z_hi: 4, z_lo: 2; z = z_hi * 2 + z_lo), core: 2. Of those that a mesh axis runs over, the one named last changes fastest.
Arguments:
- latents: bfloat16 [64, 32, 32, 640], P('dp', 'rows'), may hold values from -6 to 6
- target: bfloat16 [64, 32, 32, 640], P('dp', 'rows'), may hold values from -6 to 6
- weight: float32 [9, 640, 640], P(None, 'rows', 'dp'), may hold values from -0.078125 to 0.078125
- moment1: float32 [9, 640, 640], P(None, 'rows', 'dp'), may hold values from -6 to 6
- moment2: float32 [9, 640, 640], P(None, 'rows', 'dp'), may hold values from 0.5 to 4
Outputs:
- student: bfloat16 [64, 32, 32, 640], P('dp', 'rows')
- input_grad: bfloat16 [64, 32, 32, 640], P('dp', 'rows')
- new_weight: float32 [9, 640, 640], P(None, 'rows', 'dp')
- new_moment1: float32 [9, 640, 640], P(None, 'rows', 'dp')
- new_moment2: float32 [9, 640, 640], P(None, 'rows', 'dp')
The draws below stay inside these ranges and needn't reach their ends.
All inputs are finite; a program needn't handle non-finite values.
Results may differ from the reference program's by a relative error of at most 0.009.
Values may be sent and summed in bfloat16 or wider, within the bound.
A program may use at most 128 MiB of HBM per device.

```python
import math
import jax
import jax.numpy as jnp
from jax import lax

CH = 640
HEIGHT = 32
WIDTH = 32
B_DEV = 1
BATCH = 64
N_DP = 64
N_ROWS = 8


def shard_levels(own_key, shape, shards, low, largest):
    gain = 1.0
    for axis_at, parts in shards:
        steps = jax.random.uniform(jax.random.fold_in(jax.random.fold_in(own_key, 6), axis_at), (parts,), jnp.float32, low / len(shards), largest / len(shards))
        gain = gain * jnp.repeat(jnp.exp(steps), shape[axis_at] // parts).reshape((-1,) + (1,) * (len(shape) - 1 - axis_at))
    return gain


def scatter_about(rng, extent, deviation, reach, split=(), kind=jnp.bfloat16):
    result = deviation * jax.random.normal(rng, extent, jnp.float32)
    if split:
        result = result * shard_levels(rng, extent, split, -0.22, 0.18)
    return jnp.clip(result, -reach, reach).astype(kind)


def setup_inputs(seed: int = 0) -> dict:
    streams_of = jax.random.split(jax.random.key(seed), 6)
    return {
        "latents": scatter_about(streams_of[0], (BATCH, HEIGHT, WIDTH, CH), 1.0, 6.0, ((0, 64), (1, 8))),
        "target": scatter_about(streams_of[1], (BATCH, HEIGHT, WIDTH, CH), 1.0, 6.0, ((0, 64), (1, 8))),
        "weight": scatter_about(streams_of[2], (9, CH, CH), (9 * CH) ** -0.5, 0.078125, ((1, 8), (2, 64)), jnp.float32),
        "moment1": scatter_about(streams_of[3], (9, CH, CH), 1.0, 6.0, ((1, 8), (2, 64)), jnp.float32),
        "moment2": jnp.clip(jnp.exp(math.log(4.0) - 2.0794415 * jax.random.uniform(streams_of[4], (9, CH, CH), jnp.float32) ** shard_levels(streams_of[4], (9, CH, CH), ((1, 8), (2, 64)), -0.2, 0.2)), 0.5, 4.0),
    }


def forward_conv(padded, kernel):
    total = jnp.zeros(padded.shape[:1] + (HEIGHT, WIDTH, CH), jnp.float32)
    for tap in range(9):
        a, c = divmod(tap, 3)
        window = padded[:, a:a + HEIGHT, c:c + WIDTH].astype(jnp.float32)
        total = total + jnp.einsum('bhwc,cn->bhwn', window, kernel[tap].astype(jnp.float32))
    return total

def backward_conv(error_pad, kernel):
    total = jnp.zeros(error_pad.shape[:1] + (HEIGHT, WIDTH, CH), jnp.float32)
    for tap in range(9):
        a, c = divmod(tap, 3)
        window = error_pad[:, 2 - a:2 - a + HEIGHT, 2 - c:2 - c + WIDTH].astype(jnp.float32)
        total = total + jnp.einsum('bhwn,cn->bhwc', window, kernel[tap].astype(jnp.float32))
    return total

def reference(latents, target, weight, moment1, moment2):
    kernel = weight.astype(jnp.bfloat16)
    pad_spec = ((0, 0), (1, 1), (1, 1), (0, 0))
    padded = jnp.pad(latents, pad_spec)
    student = forward_conv(padded, kernel).astype(jnp.bfloat16)
    error = (student.astype(jnp.float32) - target.astype(jnp.float32)).astype(jnp.bfloat16)
    error_pad = jnp.pad(error, pad_spec)
    input_grad = backward_conv(error_pad, kernel).astype(jnp.bfloat16)
    band = HEIGHT // N_ROWS

    def group_step(total, group):
        start = (group * B_DEV).astype(jnp.int32)
        xs = lax.dynamic_slice_in_dim(padded, start, B_DEV, 0)
        es = lax.dynamic_slice_in_dim(error, start, B_DEV, 0).astype(jnp.float32)
        es = es.reshape(B_DEV, N_ROWS, band, WIDTH, CH)
        pieces = []
        for tap in range(9):
            a, c = divmod(tap, 3)
            window = xs[:, a:a + HEIGHT, c:c + WIDTH].astype(jnp.float32)
            window = window.reshape(B_DEV, N_ROWS, band, WIDTH, CH)
            part = jnp.einsum('bkhwc,bkhwn->kcn', window, es)
            part = part.astype(jnp.bfloat16).astype(jnp.float32)
            pieces.append(lax.optimization_barrier(jnp.sum(part, axis=0)))
        return (total + jnp.stack(pieces), None)
    summed, _ = lax.scan(group_step, jnp.zeros((9, CH, CH), jnp.float32), jnp.arange(N_DP, dtype=jnp.int32))
    grad = summed / jnp.float32(BATCH)
    new_moment1 = 0.9 * moment1 + 0.1 * grad
    new_moment2 = 0.999 * moment2 + 0.001 * grad * grad
    new_weight = weight - 0.01 * new_moment1 / (jnp.sqrt(new_moment2) + 1e-08)
    return (student, input_grad, new_weight, new_moment1, new_moment2)
```

```python
import jax
import jax.numpy as jnp
from jax import lax
from jax.sharding import PartitionSpec as P


def per_device(latents, target, weight, moment1, moment2):
    n_rows = lax.axis_size("rows")
    n_dp = lax.axis_size("dp")
    batch, band, width, ch = latents.shape
    taps, cs, ns = weight.shape
    height = band * n_rows
    cells = batch * band * width

    own = weight.astype(jnp.bfloat16).transpose(2, 0, 1).reshape(ns, taps * cs)
    kernel = lax.all_gather(own, "dp", axis=0, tiled=True)
    x = lax.all_to_all(latents, "rows", split_axis=3, concat_axis=1, tiled=True)
    pad = jnp.pad(x, ((0, 0), (1, 1), (1, 1), (0, 0)))
    wins = [pad[:, a : a + height, c : c + width] for a in range(3) for c in range(3)]
    x9 = jnp.concatenate(wins, axis=-1).reshape(batch * height * width, taps * cs)
    part = lax.dot_general(x9, kernel, (((1,), (1,)), ((), ())), preferred_element_type=jnp.float32)
    part = part.astype(jnp.bfloat16).reshape(batch, n_rows, band * width, ch)
    part = part.transpose(1, 0, 2, 3).reshape(n_rows, cells, ch)
    part = lax.all_to_all(part, "rows", 0, 0, tiled=True)
    student = jnp.sum(part.astype(jnp.float32), axis=0).astype(jnp.bfloat16)
    error = student.astype(jnp.float32) - target.reshape(cells, ch).astype(jnp.float32)
    error = error.astype(jnp.bfloat16).reshape(batch, band, width, ch)
    err = lax.all_gather(error, "rows", axis=1, tiled=True).reshape(-1, ch)
    grad = lax.dot_general(err, x9, (((0,), (0,)), ((), ())), preferred_element_type=jnp.float32)
    grad = grad.astype(jnp.bfloat16).reshape(n_dp, ns, taps * cs)
    grad = lax.all_to_all(grad, "dp", 0, 0, tiled=True)
    grad = jnp.sum(grad.astype(jnp.float32), axis=0) / jnp.float32(batch * n_dp)
    grad = grad.reshape(ns, taps, cs).transpose(1, 2, 0)
    back = jnp.dot(err, kernel, preferred_element_type=jnp.float32)
    back = back.reshape(batch, height, width, taps, cs)
    back = jnp.pad(back, ((0, 0), (1, 1), (1, 1), (0, 0), (0, 0)))
    total = None
    for tap in range(taps):
        a, c = divmod(tap, 3)
        term = back[:, 2 - a : 2 - a + height, 2 - c : 2 - c + width, tap]
        total = term if total is None else total + term
    input_grad = lax.all_to_all(
        total.astype(jnp.bfloat16), "rows", split_axis=1, concat_axis=3, tiled=True
    )
    new_moment1 = 0.9 * moment1 + 0.1 * grad
    new_moment2 = 0.999 * moment2 + 0.001 * grad * grad
    new_weight = weight - 0.01 * new_moment1 / (jnp.sqrt(new_moment2) + 1e-08)
    return (
        student.reshape(latents.shape),
        input_grad,
        new_weight,
        new_moment1,
        new_moment2,
    )


def solution(mesh):
    act = P("dp", "rows", None, None)
    par = P(None, "rows", "dp")
    return jax.shard_map(
        per_device,
        mesh=mesh,
        in_specs=(act, act, par, par, par),
        out_specs=(act, act, par, par, par),
        check_vma=False,
    )
```

```python
import jax
import jax.numpy as jnp
from jax import lax
from jax.experimental import pallas as pl
from jax.experimental.pallas import tpu as pltpu
from jax.sharding import PartitionSpec as P

MESH = pl.DeviceIdType.MESH
F32 = jnp.float32
BF16 = jnp.bfloat16
Y_ORDER = (1, 7, 2, 6, 3, 5, 4)
N_SEM = 128
NT = (((1,), (1,)), ((), ()))
TN = (((0,), (0,)), ((), ()))


def dot(a, b, dims=(((1,), (0,)), ((), ()))):
    return lax.dot_general(a, b, dims, preferred_element_type=F32)


def kernel(
    lat, tgt, wgt, stu_out, ig_out, g_out,
    kp, km, xs, st, sk, ts, tb, sb, rb, e3, gacc, ga, ra, rs, rd, ysend, yr, zs, zr,
    igp, igr, igc, ia, isum, idr, send_sem, recv_sem,
):
    dp, row = lax.axis_index("dp"), lax.axis_index("rows")
    k, y, zh = dp % 2, (dp // 2) % 8, dp // 16
    x, zl = row % 4, row // 4

    def dev(dz=0, dy=0, flip=False, dx=0, flip_zl=False):
        core = 1 - k if flip else k
        low = 1 - zl if flip_zl else zl
        return (((zh + dz) % 4 * 8 + (y + dy) % 8) * 2 + core, low * 4 + (x + dx) % 4)

    def row_dev(dr):
        return (dp, (row + dr) % 8)

    copies = []

    def send(src, dst, device):
        i = len(copies)
        copy = pltpu.make_async_remote_copy(
            src_ref=src,
            dst_ref=dst,
            send_sem=send_sem.at[i],
            recv_sem=recv_sem.at[i],
            device_id=device,
            device_id_type=MESH,
        )
        copy.start()
        copies.append(copy)
        return copy

    def lanes(j):
        return pl.ds(pl.multiple_of(j * 128, 128), 128)

    pieces = [wgt[t] for t in range(9)] + [jnp.zeros((80, 38), F32)]
    kp[x, zl, :, lanes(y)] = jnp.concatenate(pieces, axis=1).astype(BF16)
    own = kp.at[x, zl, :, lanes(y)]
    p0 = send(own, own, dev(flip_zl=True))
    up0 = send(lat.at[0:64], xs.at[3, 32:96], dev(dz=1))
    dn1 = send(lat.at[64:128], xs.at[1, 96:160], dev(dz=-1))
    up1 = send(lat.at[64:128], xs.at[3, 96:160], dev(dz=1))
    dn0 = send(lat.at[0:64], xs.at[1, 32:96], dev(dz=-1))
    part = [send(lat, xs.at[4, 32:160], dev(flip=True))]
    top = [send(lat.at[0:32], xs.at[0, 160:192], row_dev(-1))]
    bot = [send(lat.at[96:128], xs.at[0, 0:32], row_dev(1))]
    xs[0, 32:160] = lat[...]

    p0.wait_recv()
    block = kp.at[x, :, :, lanes(y)]
    p1 = {dy: send(block, block, dev(dy=dy)) for dy in Y_ORDER}
    right, left, fwd_r, fwd_l = {}, {}, {}, {}
    right[0] = send(block, block, dev(dx=1))
    left[0] = send(block, block, dev(dx=-1))

    lane = lax.broadcasted_iota(jnp.int32, (640, 128), 1)
    chan = lax.broadcasted_iota(jnp.int32, (640, 128), 0)
    place = lane + 10 * ((lane * 205) >> 11)
    for s in range(8):
        core = k if s < 4 else 1 - k
        hit = (chan == place + (zh + s % 4) % 4 * 160 + core * 10) & (lane < 80)
        st[:, s * 128 : s * 128 + 128] = jnp.where(hit, 1.0, 0.0).astype(BF16)

    def halos(s):
        top.append(send(xs.at[s, 32:64], xs.at[s, 160:192], row_dev(-1)))
        bot.append(send(xs.at[s, 128:160], xs.at[s, 0:32], row_dev(1)))

    up0.wait_recv()
    over0 = send(xs.at[3, 32:96], xs.at[2, 32:96], dev(dz=1))
    dn1.wait_recv()
    over1 = send(xs.at[1, 96:160], xs.at[2, 96:160], dev(dz=-1))

    def y_step(dy):
        p1[dy].wait_recv()
        got = kp.at[x, :, :, lanes((y - dy) % 8)]
        right[dy] = send(got, got, dev(dx=1))
        left[dy] = send(got, got, dev(dx=-1))

    def x_step(dy):
        right[dy].wait_recv()
        got = kp.at[(x + 3) % 4, 0, :, lanes((y - dy) % 8)]
        fwd_r[dy] = send(got, got, dev(dx=1))
        left[dy].wait_recv()
        got = kp.at[(x + 1) % 4, 1, :, lanes((y - dy) % 8)]
        fwd_l[dy] = send(got, got, dev(dx=-1))

    y_step(1)
    y_step(7)
    x_step(0)
    up1.wait_recv()
    halos(3)
    part.append(send(xs.at[3, 32:160], xs.at[7, 32:160], dev(flip=True)))
    dn0.wait_recv()
    halos(1)
    part.append(send(xs.at[1, 32:160], xs.at[5, 32:160], dev(flip=True)))
    y_step(2)
    y_step(6)
    x_step(1)
    x_step(7)

    ts[...] = dot(tgt[...], st[...]).astype(BF16)
    tsent = []
    for s in (4, 1, 3, 5, 7, 2, 6):
        back = s // 4 * 4 + (-s) % 4
        src = ts.at[:, s * 128 : s * 128 + 128]
        tsent.append(send(src, tb.at[back], dev(dz=s % 4, flip=s >= 4)))
    tb[0] = ts[:, 0:128]

    y_step(3)
    y_step(5)
    y_step(4)
    x_step(2)
    x_step(6)
    over0.wait_recv()
    over1.wait_recv()
    halos(2)
    part.append(send(xs.at[2, 32:160], xs.at[6, 32:160], dev(flip=True)))
    x_step(3)
    x_step(5)
    x_step(4)

    l0 = lax.broadcasted_iota(jnp.int32, (128, 768), 0)
    q = lax.broadcasted_iota(jnp.int32, (128, 768), 1)
    tap = (l0 * 205) >> 11
    third = (tap * 11) >> 5
    want = third * 256 + (tap - 3 * third) * 80 + l0 - 10 * tap
    diff = jnp.where(l0 < 90, q - want, -1)

    def make_sk(j, carry):
        hit = jnp.where(diff == j * 10, 1.0, 0.0)
        sk[pl.ds(pl.multiple_of(j * 128, 128), 128), :] = hit.astype(BF16)
        return carry

    lax.fori_loop(0, 8, make_sk, 0)

    def place_kernel(dx):
        at = (x + dx) % 4
        out = dot(kp[at].reshape(160, 1024), sk[...]).astype(BF16)
        km[pl.ds(pl.multiple_of(at * 80, 16), 80), :] = out[:80]
        km[pl.ds(pl.multiple_of(320 + at * 80, 16), 80), :] = out[80:]

    place_kernel(0)
    place_kernel(1)
    place_kernel(3)

    for c in top + bot:
        c.wait_recv()
    part.append(send(xs.at[0:4, 0:32], xs.at[4:8, 0:32], dev(flip=True)))
    part.append(send(xs.at[0:4, 160:192], xs.at[4:8, 160:192], dev(flip=True)))
    for dy in (0,) + Y_ORDER:
        fwd_r[dy].wait_recv()
        fwd_l[dy].wait_recv()
    place_kernel(2)
    for c in part:
        c.wait_recv()
    part[-1].wait_send()
    part[-2].wait_send()

    @pl.when(row == 0)
    def _():
        xs[:, 0:32, :] = jnp.zeros((8, 32, 640), BF16)

    @pl.when(row == 7)
    def _():
        xs[:, 160:192, :] = jnp.zeros((8, 32, 640), BF16)

    for c in tsent:
        c.wait_recv()

    col = lax.broadcasted_iota(jnp.int32, (256, 128), 0) % 32
    first, last = col == 0, col == 31
    real = lax.broadcasted_iota(jnp.int32, (256, 128), 1) < 80

    def forward(m, carry):
        two = pl.ds(2 * m, 2)
        acc = None
        for a in range(3):
            win = xs[two, 32 * a : 32 * a + 128, :].reshape(256, 640)
            term = dot(win, km[:, 256 * a : 256 * a + 256])
            acc = term if acc is None else acc + term
        mid = pltpu.roll(acc, 176, 1)[:, :128]
        end = pltpu.roll(acc, 96, 1)[:, :128]
        total = mid + jnp.where(first, 0.0, pltpu.roll(acc[:, :128], 1, 0))
        total = total + jnp.where(last, 0.0, pltpu.roll(end, 255, 0))
        stu = jnp.where(real, total, 0.0).astype(BF16)
        sb[two] = stu.reshape(2, 128, 128)
        err = stu.astype(F32) - tb[two].reshape(256, 128).astype(F32)
        err = err.astype(BF16).astype(F32)
        zero = jnp.zeros((256, 128), F32)
        nxt = jnp.where(last, 0.0, pltpu.roll(err, 255, 0))
        prv = jnp.where(first, 0.0, pltpu.roll(err, 1, 0))
        wide = jnp.concatenate([nxt, zero], axis=1)
        wide = wide + pltpu.roll(jnp.concatenate([err, zero], axis=1), 80, 1)
        wide = wide + pltpu.roll(jnp.concatenate([prv, zero], axis=1), 160, 1)
        e3[two, 32:160, :] = wide.astype(BF16).reshape(2, 128, 256)
        return carry

    lax.fori_loop(0, 4, forward, 0)

    etop = send(e3.at[:, 32:64], e3.at[:, 160:192], row_dev(-1))
    ebot = send(e3.at[:, 128:160], e3.at[:, 0:32], row_dev(1))
    ssent = []
    for s in (4, 1, 3, 5, 7, 2, 6):
        back = s // 4 * 4 + (-s) % 4
        dst = rb.at[:, back * 128 : back * 128 + 128]
        ssent.append(send(sb.at[s], dst, dev(dz=s % 4, flip=s >= 4)))
    rb[:, 0:128] = sb[0]

    gacc[...] = jnp.zeros((640, 768), F32)

    def weight_grad(m, carry):
        two = pl.ds(2 * m, 2)
        errs = e3[two, 32:160, :].reshape(256, 256)
        for a in range(3):
            win = xs[two, 32 * a : 32 * a + 128, :].reshape(256, 640)
            gacc[:, 256 * a : 256 * a + 256] += dot(win, errs, TN)
        return carry

    lax.fori_loop(0, 4, weight_grad, 0)

    def place_grad(dx):
        at = (x + dx) % 4
        low = gacc[pl.ds(pl.multiple_of(at * 80, 8), 80), :]
        high = gacc[pl.ds(pl.multiple_of(320 + at * 80, 8), 80), :]
        both = jnp.concatenate([low, high], axis=0).astype(BF16)
        ga[dx] = dot(both, sk[...], NT).astype(BF16).reshape(2, 80, 1024)

    place_grad(2)
    gr_a = send(ga.at[2, 0], ra.at[0], dev(dx=1))
    gr_b = send(ga.at[2, 1], ra.at[1], dev(dx=-1))
    place_grad(1)
    gd_a = send(ga.at[1, 1], rd.at[1], dev(dx=1))
    place_grad(3)
    gd_b = send(ga.at[3, 0], rd.at[0], dev(dx=-1))
    place_grad(0)

    etop.wait_recv()
    ebot.wait_recv()
    etop.wait_send()
    ebot.wait_send()

    @pl.when(row == 0)
    def _():
        e3[:, 0:32, :] = jnp.zeros((8, 32, 256), BF16)

    @pl.when(row == 7)
    def _():
        e3[:, 160:192, :] = jnp.zeros((8, 32, 256), BF16)

    def input_grad(m, carry):
        two = pl.ds(2 * m, 2)
        acc = None
        for a in range(3):
            win = e3[two, 64 - 32 * a : 192 - 32 * a, :].reshape(256, 256)
            term = dot(win, km[:, 256 * a : 256 * a + 256], NT)
            acc = term if acc is None else acc + term
        igp[two] = acc.astype(BF16).reshape(2, 128, 640)
        return carry

    lax.fori_loop(2, 4, input_grad, 0)
    ip = send(igp.at[4:8], igr, dev(flip=True))
    gr_a.wait_recv()
    rs[0] = (ra[0].astype(F32) + ga[1, 0].astype(F32)).astype(BF16)
    gs_a = send(rs.at[0], rd.at[2], dev(dx=1))
    gr_b.wait_recv()
    rs[1] = (ra[1].astype(F32) + ga[3, 1].astype(F32)).astype(BF16)
    gs_b = send(rs.at[1], rd.at[3], dev(dx=-1))
    lax.fori_loop(0, 2, input_grad, 0)
    ip.wait_recv()
    for s in (2, 1, 3, 0):
        igc[s] = (igp[s].astype(F32) + igr[s].astype(F32)).astype(BF16)
        if s == 2:
            ir_a = send(igc.at[2, 0:64], ia.at[0], dev(dz=1))
            ir_b = send(igc.at[2, 64:128], ia.at[1], dev(dz=-1))
        if s == 1:
            id_a = send(igc.at[1, 64:128], idr.at[1], dev(dz=1))
        if s == 3:
            id_b = send(igc.at[3, 0:64], idr.at[0], dev(dz=-1))

    for c in (gd_a, gd_b, gs_a, gs_b):
        c.wait_recv()
    low = ga[0, 0].astype(F32) + rd[0].astype(F32) + rd[2].astype(F32)
    high = ga[0, 1].astype(F32) + rd[1].astype(F32) + rd[3].astype(F32)
    ysend[0] = low.astype(BF16)
    ysend[1] = high.astype(BF16)
    ysent = []
    for i, dy in enumerate(Y_ORDER):
        src = ysend.at[:, :, lanes((y + dy) % 8)]
        ysent.append(send(src, yr.at[i], dev(dy=dy)))

    ir_a.wait_recv()
    isum[0] = (ia[0].astype(F32) + igc[1, 0:64].astype(F32)).astype(BF16)
    is_a = send(isum.at[0], idr.at[2], dev(dz=1))
    ir_b.wait_recv()
    isum[1] = (ia[1].astype(F32) + igc[3, 64:128].astype(F32)).astype(BF16)
    is_b = send(isum.at[1], idr.at[3], dev(dz=-1))

    for c in ssent:
        c.wait_recv()
    stu_out[...] = dot(rb[...], st[...], NT).astype(BF16)

    total = ysend[:, :, lanes(y)].astype(F32)
    for i in range(7):
        ysent[i].wait_recv()
        total = total + yr[i].astype(F32)
    zs[...] = total
    zc = send(zs.at[1 - zl], zr, dev(flip_zl=True))

    for c in (id_a, id_b, is_a, is_b):
        c.wait_recv()
    low = igc[0, 0:64].astype(F32) + idr[0].astype(F32) + idr[2].astype(F32)
    high = igc[0, 64:128].astype(F32) + idr[1].astype(F32) + idr[3].astype(F32)
    ig_out[0:64] = low.astype(BF16)
    ig_out[64:128] = high.astype(BF16)

    zc.wait_recv()
    grad = (zs[zl] + zr[...]) * (1.0 / 64.0)
    for t in range(9):
        g_out[t] = grad[:, 10 * t : 10 * t + 10]
    waited = (part[-1], part[-2], etop, ebot)
    for c in copies:
        if not any(c is w for w in waited):
            c.wait_send()


def per_device(latents, target, weight, moment1, moment2):
    vmem = pl.BlockSpec(memory_space=pltpu.VMEM)
    student, input_grad, grad = pl.pallas_call(
        kernel,
        out_shape=(
            jax.ShapeDtypeStruct((128, 640), BF16),
            jax.ShapeDtypeStruct((128, 640), BF16),
            jax.ShapeDtypeStruct((9, 80, 10), F32),
        ),
        in_specs=[vmem] * 3,
        out_specs=(vmem,) * 3,
        scratch_shapes=[
            pltpu.VMEM((4, 2, 80, 1024), BF16),
            pltpu.VMEM((640, 768), BF16),
            pltpu.VMEM((8, 192, 640), BF16),
            pltpu.VMEM((640, 1024), BF16),
            pltpu.VMEM((1024, 768), BF16),
            pltpu.VMEM((128, 1024), BF16),
            pltpu.VMEM((8, 128, 128), BF16),
            pltpu.VMEM((8, 128, 128), BF16),
            pltpu.VMEM((128, 1024), BF16),
            pltpu.VMEM((8, 192, 256), BF16),
            pltpu.VMEM((640, 768), F32),
            pltpu.VMEM((4, 2, 80, 1024), BF16),
            pltpu.VMEM((2, 80, 1024), BF16),
            pltpu.VMEM((2, 80, 1024), BF16),
            pltpu.VMEM((4, 80, 1024), BF16),
            pltpu.VMEM((2, 80, 1024), BF16),
            pltpu.VMEM((7, 2, 80, 128), BF16),
            pltpu.VMEM((2, 80, 128), F32),
            pltpu.VMEM((80, 128), F32),
            pltpu.VMEM((8, 128, 640), BF16),
            pltpu.VMEM((4, 128, 640), BF16),
            pltpu.VMEM((4, 128, 640), BF16),
            pltpu.VMEM((2, 64, 640), BF16),
            pltpu.VMEM((2, 64, 640), BF16),
            pltpu.VMEM((4, 64, 640), BF16),
            pltpu.SemaphoreType.DMA((N_SEM,)),
            pltpu.SemaphoreType.DMA((N_SEM,)),
        ],
        compiler_params=pltpu.CompilerParams(has_side_effects=True, vmem_limit_bytes=48 << 20),
    )(latents.reshape(128, 640), target.reshape(128, 640), weight)
    new_moment1 = 0.9 * moment1 + 0.1 * grad
    new_moment2 = 0.999 * moment2 + 0.001 * grad * grad
    new_weight = weight - 0.01 * new_moment1 / (jnp.sqrt(new_moment2) + 1e-08)
    return (
        student.reshape(latents.shape),
        input_grad.reshape(latents.shape),
        new_weight,
        new_moment1,
        new_moment2,
    )


def solution(mesh):
    act = P("dp", "rows", None, None)
    par = P(None, "rows", "dp")
    return jax.shard_map(
        per_device,
        mesh=mesh,
        in_specs=(act, act, par, par, par),
        out_specs=(act, act, par, par, par),
        check_vma=False,
    )
```

```python
import jax
import jax.numpy as jnp
from jax import lax
from jax.experimental import pallas as pl
from jax.experimental.pallas import tpu as pltpu
from jax.sharding import PartitionSpec as P

MESH = pl.DeviceIdType.MESH
F32 = jnp.float32
BF16 = jnp.bfloat16
Y_ORDER = (1, 7, 2, 6, 3, 5, 4)
BLOCKS = (4, 3, 5, 2, 6, 1, 7, 0)
GROUPS = ((0, 384), (384, 640), (640, 1024))
N_SEM = 128
NT = (((1,), (1,)), ((), ()))
TN = (((0,), (0,)), ((), ()))


class Copy:
    def __init__(self, copy):
        self.copy, self.got, self.gone = copy, False, False
        copy.start()

    def recv(self):
        if not self.got:
            self.copy.wait_recv()
        self.got = True

    def sent(self):
        if not self.gone:
            self.copy.wait_send()
        self.gone = True


def dot(a, b, dims=(((1,), (0,)), ((), ()))):
    return lax.dot_general(a, b, dims, preferred_element_type=F32)


def kernel(
    lat, tgt, wgt, stu_out, ig_out, g_out,
    kp, km, xs, st, sk, ts, tb, tr, sb, rb, e3, gacc, gb, ga, ra, rs, rd, ysend, yr, zs, zr,
    igp, igr, igc, ia, isum, idr, send_sem, recv_sem,
):
    dp, row = lax.axis_index("dp"), lax.axis_index("rows")
    k, y, zh = dp % 2, (dp // 2) % 8, dp // 16
    x, zl = row % 4, row // 4

    def dev(dz=0, dy=0, flip=False, dx=0, flip_zl=False):
        core = 1 - k if flip else k
        low = 1 - zl if flip_zl else zl
        return (((zh + dz) % 4 * 8 + (y + dy) % 8) * 2 + core, low * 4 + (x + dx) % 4)

    def row_dev(dr):
        return (dp, (row + dr) % 8)

    copies = []

    def send(src, dst, device):
        i = len(copies)
        copy = pltpu.make_async_remote_copy(
            src_ref=src,
            dst_ref=dst,
            send_sem=send_sem.at[i],
            recv_sem=recv_sem.at[i],
            device_id=device,
            device_id_type=MESH,
        )
        copies.append(Copy(copy))
        return copies[i]

    def blk(dy):
        j = BLOCKS.index(dy % 8)
        return slice(j * 128, j * 128 + 128)

    def rows_of(dx, low):
        at = (zl if low == 0 else 1 - zl) * 4 + (x + dx) % 4
        return pl.ds(pl.multiple_of(at * 80, 16), 80)

    barrier = pltpu.get_barrier_semaphore()
    partners = [dev(flip_zl=True), dev(dx=1), dev(dx=-1), row_dev(1), row_dev(-1)]
    partners += [dev(dy=dy) for dy in Y_ORDER] + [dev(dz=dz) for dz in (1, 2, 3)]
    partners += [dev(dz=dz, flip=True) for dz in range(4)]
    for partner in partners:
        pl.semaphore_signal(barrier, inc=1, device_id=partner, device_id_type=MESH)

    fill = jnp.zeros((6, 80), F32)
    rows = jnp.concatenate([v for t in range(9) for v in (wgt[t], fill)], axis=0)
    l9 = lax.broadcasted_iota(jnp.int32, (144, 128), 1)
    n9 = lax.broadcasted_iota(jnp.int32, (144, 128), 0)
    pick = (n9 & 15 < 10) & (l9 == (n9 >> 4) * 10 + (n9 & 15))
    pick = jnp.where(pick, 1.0, 0.0).astype(BF16)
    kp[0, 0, :, blk(0)] = dot(rows.astype(BF16), pick, TN).astype(BF16)
    xs[0, 32:160] = lat[...]
    lane = lax.broadcasted_iota(jnp.int32, (640, 128), 1)
    chan = lax.broadcasted_iota(jnp.int32, (640, 128), 0)
    place = lane + 10 * ((lane * 205) >> 11)
    for s in range(8):
        core = k if s < 4 else 1 - k
        hit = (chan == place + (zh + s % 4) % 4 * 160 + core * 10) & (lane < 80)
        st[:, s * 128 : s * 128 + 128] = jnp.where(hit, 1.0, 0.0).astype(BF16)

    l0 = lax.broadcasted_iota(jnp.int32, (128, 768), 0)
    q = lax.broadcasted_iota(jnp.int32, (128, 768), 1)
    tap = (l0 * 205) >> 11
    third = (tap * 11) >> 5
    want = third * 256 + (tap - 3 * third) * 80 + l0 - 10 * tap
    diff = jnp.where(l0 < 90, q - want, -1)
    for j, dy in enumerate(BLOCKS):
        hit = jnp.where(diff == (y + dy) % 8 * 10, 1.0, 0.0)
        sk[j * 128 : j * 128 + 128, :] = hit.astype(BF16)

    pl.semaphore_wait(barrier, len(partners))
    p0 = send(kp.at[0, 0, :, blk(0)], kp.at[0, 1, :, blk(0)], dev(flip_zl=True))
    up0 = send(lat.at[0:64], xs.at[3, 32:96], dev(dz=1))
    dn1 = send(lat.at[64:128], xs.at[1, 96:160], dev(dz=-1))
    up1 = send(lat.at[64:128], xs.at[3, 96:160], dev(dz=1))
    dn0 = send(lat.at[0:64], xs.at[1, 32:96], dev(dz=-1))
    part = [send(lat, xs.at[4, 32:160], dev(flip=True))]
    top = [send(lat.at[0:32], xs.at[0, 160:192], row_dev(-1))]
    bot = [send(lat.at[96:128], xs.at[0, 0:32], row_dev(1))]

    p0.recv()
    block = kp.at[0, :, :, blk(0)]
    p1 = {dy: send(block, kp.at[0, :, :, blk(-dy)], dev(dy=dy)) for dy in Y_ORDER}
    right, left, fwd_r, fwd_l = {}, {}, {}, {}
    right[0] = send(block, kp.at[3, :, :, blk(0)], dev(dx=1))
    left[0] = send(block, kp.at[1, :, :, blk(0)], dev(dx=-1))

    def halos(s):
        top.append(send(xs.at[s, 32:64], xs.at[s, 160:192], row_dev(-1)))
        bot.append(send(xs.at[s, 128:160], xs.at[s, 0:32], row_dev(1)))

    up0.recv()
    over0 = send(xs.at[3, 32:96], xs.at[2, 32:96], dev(dz=1))
    dn1.recv()
    over1 = send(xs.at[1, 96:160], xs.at[2, 96:160], dev(dz=-1))

    def y_step(dy):
        p1[dy].recv()
        got = kp.at[0, :, :, blk(-dy)]
        right[dy] = send(got, kp.at[3, :, :, blk(-dy)], dev(dx=1))
        left[dy] = send(got, kp.at[1, :, :, blk(-dy)], dev(dx=-1))

    def x_step(dy):
        right[dy].recv()
        dst = kp.at[2, 0, :, blk(-dy)]
        fwd_r[dy] = send(kp.at[3, 0, :, blk(-dy)], dst, dev(dx=1))
        left[dy].recv()
        dst = kp.at[2, 1, :, blk(-dy)]
        fwd_l[dy] = send(kp.at[1, 1, :, blk(-dy)], dst, dev(dx=-1))

    y_step(1)
    y_step(7)
    x_step(0)
    up1.recv()
    halos(3)
    part.append(send(xs.at[3, 32:160], xs.at[7, 32:160], dev(flip=True)))
    dn0.recv()
    halos(1)
    part.append(send(xs.at[1, 32:160], xs.at[5, 32:160], dev(flip=True)))
    y_step(2)
    y_step(6)
    x_step(1)
    x_step(7)

    ts[...] = dot(st[...], tgt[...], (((0,), (1,)), ((), ()))).astype(BF16)
    tsent = []
    for s in (4, 1, 3, 5, 7):
        back = s // 4 * 4 + (-s) % 4
        src = ts.at[s * 128 : s * 128 + 80]
        tsent.append(send(src, tb.at[back], dev(dz=s % 4, flip=s >= 4)))
    two_up = send(ts.at[256:336], tr.at[0], dev(dz=1))
    two_dn = send(ts.at[768:848], tr.at[1], dev(dz=-1))
    tb[0] = ts[0:80]

    y_step(3)
    y_step(5)
    y_step(4)
    x_step(2)
    x_step(6)
    over0.recv()
    over1.recv()
    halos(2)
    part.append(send(xs.at[2, 32:160], xs.at[6, 32:160], dev(flip=True)))
    two_up.recv()
    tsent.append(send(tr.at[0], tb.at[2], dev(dz=1)))
    two_dn.recv()
    tsent.append(send(tr.at[1], tb.at[6], dev(dz=-1, flip=True)))
    x_step(3)
    x_step(5)
    x_step(4)

    def place_kernel(dx):
        out = dot(kp[dx].reshape(160, 1024), sk[...]).astype(BF16)
        km[rows_of(dx, 0), :] = out[:80]
        km[rows_of(dx, 1), :] = out[80:]

    place_kernel(0)
    place_kernel(1)
    place_kernel(3)

    for c in top + bot:
        c.recv()
    part.append(send(xs.at[0:4, 0:32], xs.at[4:8, 0:32], dev(flip=True)))
    part.append(send(xs.at[0:4, 160:192], xs.at[4:8, 160:192], dev(flip=True)))
    for dy in (0,) + Y_ORDER:
        fwd_r[dy].recv()
        fwd_l[dy].recv()
    place_kernel(2)
    for c in part:
        c.recv()
    part[-1].sent()
    part[-2].sent()

    @pl.when(row == 0)
    def _():
        xs[:, 0:32, :] = jnp.zeros((8, 32, 640), BF16)

    @pl.when(row == 7)
    def _():
        xs[:, 160:192, :] = jnp.zeros((8, 32, 640), BF16)

    for c in tsent:
        c.recv()

    col = lax.broadcasted_iota(jnp.int32, (256, 128), 0) % 32
    first, last = col == 0, col == 31
    real = lax.broadcasted_iota(jnp.int32, (256, 128), 1) < 80

    def forward(m, carry):
        two = pl.ds(2 * m, 2)
        acc = None
        for a in range(3):
            win = xs[two, 32 * a : 32 * a + 128, :].reshape(256, 640)
            term = dot(win, km[:, 256 * a : 256 * a + 256])
            acc = term if acc is None else acc + term
        mid = pltpu.roll(acc, 176, 1)[:, :128]
        end = pltpu.roll(acc, 96, 1)[:, :128]
        total = mid + jnp.where(first, 0.0, pltpu.roll(acc[:, :128], 1, 0))
        total = total + jnp.where(last, 0.0, pltpu.roll(end, 255, 0))
        stu = jnp.where(real, total, 0.0).astype(BF16)
        sb[two] = stu.reshape(2, 128, 128)
        pair, fill = tb[two].astype(F32), jnp.zeros((48, 128), F32)
        goal = [jnp.concatenate([pair[i], fill], axis=0).T for i in range(2)]
        err = stu.astype(F32) - jnp.concatenate(goal, axis=0)
        err = err.astype(BF16).astype(F32)
        zero = jnp.zeros((256, 128), F32)
        nxt = jnp.where(last, 0.0, pltpu.roll(err, 255, 0))
        prv = jnp.where(first, 0.0, pltpu.roll(err, 1, 0))
        wide = jnp.concatenate([nxt, zero], axis=1)
        wide = wide + pltpu.roll(jnp.concatenate([err, zero], axis=1), 80, 1)
        wide = wide + pltpu.roll(jnp.concatenate([prv, zero], axis=1), 160, 1)
        e3[two, 32:160, :] = wide.astype(BF16).reshape(2, 128, 256)
        return carry

    lax.fori_loop(0, 4, forward, 0)

    etop = send(e3.at[:, 32:64], e3.at[:, 160:192], row_dev(-1))
    ebot = send(e3.at[:, 128:160], e3.at[:, 0:32], row_dev(1))
    ssent = []
    for s in (4, 1, 3, 5, 7, 2, 6):
        back = s // 4 * 4 + (-s) % 4
        dst = rb.at[:, back * 128 : back * 128 + 128]
        ssent.append(send(sb.at[s], dst, dev(dz=s % 4, flip=s >= 4)))
    rb[:, 0:128] = sb[0]

    gacc[...] = jnp.zeros((640, 768), F32)

    def weight_grad(m, carry):
        two = pl.ds(2 * m, 2)
        errs = e3[two, 32:160, :].reshape(256, 256)
        for a in range(3):
            win = xs[two, 32 * a : 32 * a + 128, :].reshape(256, 640)
            gacc[:, 256 * a : 256 * a + 256] += dot(win, errs, TN)
        return carry

    lax.fori_loop(0, 4, weight_grad, 0)
    gb[...] = gacc[...].astype(BF16)

    first_hop, raw, second_hop = [], [], []
    for lo, hi in GROUPS:
        cols = slice(lo, hi)
        ga[:, cols] = dot(gb[...], sk[cols, :], NT).astype(BF16)
        up = send(ga.at[rows_of(2, 0), cols], ra.at[0, :, cols], dev(dx=1))
        dn = send(ga.at[rows_of(2, 1), cols], ra.at[1, :, cols], dev(dx=-1))
        first_hop.append((up, dn))
        up = send(ga.at[rows_of(1, 1), cols], rd.at[1, :, cols], dev(dx=1))
        dn = send(ga.at[rows_of(3, 0), cols], rd.at[0, :, cols], dev(dx=-1))
        raw.append((up, dn))

    def relay(g):
        cols = slice(*GROUPS[g])
        up, dn = first_hop[g]
        up.recv()
        rs[0, :, cols] = (ra[0, :, cols].astype(F32) + ga[rows_of(1, 0), cols].astype(F32)).astype(BF16)
        up = send(rs.at[0, :, cols], rd.at[2, :, cols], dev(dx=1))
        dn.recv()
        rs[1, :, cols] = (ra[1, :, cols].astype(F32) + ga[rows_of(3, 1), cols].astype(F32)).astype(BF16)
        dn = send(rs.at[1, :, cols], rd.at[3, :, cols], dev(dx=-1))
        second_hop.append((up, dn))

    ysent = []

    def spread(g):
        cols = slice(*GROUPS[g])
        for c in raw[g] + second_hop[g]:
            c.recv()
        for i in range(2):
            mine = ga[rows_of(0, i), cols].astype(F32)
            both = rd[i, :, cols].astype(F32) + rd[i + 2, :, cols].astype(F32)
            ysend[i, :, cols] = (mine + both).astype(BF16)
        for dy in BLOCKS[GROUPS[g][0] // 128 : GROUPS[g][1] // 128]:
            if dy:
                ysent.append(send(ysend.at[:, :, blk(dy)], yr.at[len(ysent)], dev(dy=dy)))

    etop.recv()
    ebot.recv()
    etop.sent()
    ebot.sent()

    @pl.when(row == 0)
    def _():
        e3[:, 0:32, :] = jnp.zeros((8, 32, 256), BF16)

    @pl.when(row == 7)
    def _():
        e3[:, 160:192, :] = jnp.zeros((8, 32, 256), BF16)

    def input_grad(m, carry):
        two = pl.ds(2 * m, 2)
        acc = None
        for a in range(3):
            win = e3[two, 64 - 32 * a : 192 - 32 * a, :].reshape(256, 256)
            term = dot(win, km[:, 256 * a : 256 * a + 256], NT)
            acc = term if acc is None else acc + term
        igp[two] = acc.astype(BF16).reshape(2, 128, 640)
        return carry

    lax.fori_loop(2, 3, input_grad, 0)
    relay(0)
    lax.fori_loop(3, 4, input_grad, 0)
    ip = send(igp.at[4:8], igr, dev(flip=True))
    relay(1)
    lax.fori_loop(0, 1, input_grad, 0)
    relay(2)
    spread(0)
    lax.fori_loop(1, 2, input_grad, 0)
    spread(1)
    ip.recv()
    for s in (2, 1, 3, 0):
        igc[s] = (igp[s].astype(F32) + igr[s].astype(F32)).astype(BF16)
        if s == 2:
            ir_a = send(igc.at[2, 0:64], ia.at[0], dev(dz=1))
            ir_b = send(igc.at[2, 64:128], ia.at[1], dev(dz=-1))
        if s == 1:
            id_a = send(igc.at[1, 64:128], idr.at[1], dev(dz=1))
        if s == 3:
            id_b = send(igc.at[3, 0:64], idr.at[0], dev(dz=-1))
    spread(2)

    ir_a.recv()
    isum[0] = (ia[0].astype(F32) + igc[1, 0:64].astype(F32)).astype(BF16)
    is_a = send(isum.at[0], idr.at[2], dev(dz=1))
    ir_b.recv()
    isum[1] = (ia[1].astype(F32) + igc[3, 64:128].astype(F32)).astype(BF16)
    is_b = send(isum.at[1], idr.at[3], dev(dz=-1))

    for c in ssent:
        c.recv()
    stu_out[...] = dot(rb[...], st[...], NT).astype(BF16)

    total = ysend[:, :, blk(0)].astype(F32)
    for i in range(7):
        ysent[i].recv()
        total = total + yr[i].astype(F32)
    zs[...] = total
    zc = send(zs.at[1], zr, dev(flip_zl=True))

    for c in (id_a, id_b, is_a, is_b):
        c.recv()
    low = igc[0, 0:64].astype(F32) + idr[0].astype(F32) + idr[2].astype(F32)
    high = igc[0, 64:128].astype(F32) + idr[1].astype(F32) + idr[3].astype(F32)
    ig_out[0:64] = low.astype(BF16)
    ig_out[64:128] = high.astype(BF16)

    zc.recv()
    grad = (zs[0] + zr[...]) * (1.0 / 64.0)
    turned = jnp.concatenate([grad, jnp.zeros((48, 128), F32)], axis=0).T
    for t in range(9):
        g_out[t] = turned[10 * t : 10 * t + 10, :80]
    for c in copies:
        c.sent()


def per_device(latents, target, weight, moment1, moment2):
    vmem = pl.BlockSpec(memory_space=pltpu.VMEM)
    student, input_grad, grad = pl.pallas_call(
        kernel,
        out_shape=(
            jax.ShapeDtypeStruct((128, 640), BF16),
            jax.ShapeDtypeStruct((128, 640), BF16),
            jax.ShapeDtypeStruct((9, 10, 80), F32),
        ),
        in_specs=[vmem] * 3,
        out_specs=(vmem,) * 3,
        scratch_shapes=[
            pltpu.VMEM((4, 2, 80, 1024), BF16),
            pltpu.VMEM((640, 768), BF16),
            pltpu.VMEM((8, 192, 640), BF16),
            pltpu.VMEM((640, 1024), BF16),
            pltpu.VMEM((1024, 768), BF16),
            pltpu.VMEM((1024, 128), BF16),
            pltpu.VMEM((8, 80, 128), BF16),
            pltpu.VMEM((2, 80, 128), BF16),
            pltpu.VMEM((8, 128, 128), BF16),
            pltpu.VMEM((128, 1024), BF16),
            pltpu.VMEM((8, 192, 256), BF16),
            pltpu.VMEM((640, 768), F32),
            pltpu.VMEM((640, 768), BF16),
            pltpu.VMEM((640, 1024), BF16),
            pltpu.VMEM((2, 80, 1024), BF16),
            pltpu.VMEM((2, 80, 1024), BF16),
            pltpu.VMEM((4, 80, 1024), BF16),
            pltpu.VMEM((2, 80, 1024), BF16),
            pltpu.VMEM((7, 2, 80, 128), BF16),
            pltpu.VMEM((2, 80, 128), F32),
            pltpu.VMEM((80, 128), F32),
            pltpu.VMEM((8, 128, 640), BF16),
            pltpu.VMEM((4, 128, 640), BF16),
            pltpu.VMEM((4, 128, 640), BF16),
            pltpu.VMEM((2, 64, 640), BF16),
            pltpu.VMEM((2, 64, 640), BF16),
            pltpu.VMEM((4, 64, 640), BF16),
            pltpu.SemaphoreType.DMA((N_SEM,)),
            pltpu.SemaphoreType.DMA((N_SEM,)),
        ],
        compiler_params=pltpu.CompilerParams(
            collective_id=0, has_side_effects=True, vmem_limit_bytes=48 << 20
        ),
    )(latents.reshape(128, 640), target.reshape(128, 640), weight.transpose(0, 2, 1))
    grad = grad.transpose(0, 2, 1)
    new_moment1 = 0.9 * moment1 + 0.1 * grad
    new_moment2 = 0.999 * moment2 + 0.001 * grad * grad
    new_weight = weight - 0.01 * new_moment1 / (jnp.sqrt(new_moment2) + 1e-08)
    return (
        student.reshape(latents.shape),
        input_grad.reshape(latents.shape),
        new_weight,
        new_moment1,
        new_moment2,
    )


def solution(mesh):
    act = P("dp", "rows", None, None)
    par = P(None, "rows", "dp")
    return jax.shard_map(
        per_device,
        mesh=mesh,
        in_specs=(act, act, par, par, par),
        out_specs=(act, act, par, par, par),
        check_vma=False,
    )
```

```python
import jax
import jax.numpy as jnp
from jax import lax
from jax.experimental import pallas as pl
from jax.experimental.pallas import tpu as pltpu
from jax.sharding import PartitionSpec as P

MESH = pl.DeviceIdType.MESH
F32 = jnp.float32
BF16 = jnp.bfloat16
Y_ORDER = (1, 7, 2, 6, 3, 5, 4)
BLOCKS = (4, 3, 5, 2, 6, 1, 7, 0)
GROUPS = ((0, 384), (384, 640), (640, 1024))
N_SEM = 160
NT = (((1,), (1,)), ((), ()))
TN = (((0,), (0,)), ((), ()))


class Copy:
    def __init__(self, copy):
        self.copy, self.got, self.gone = copy, False, False
        copy.start()

    def recv(self):
        if not self.got:
            self.copy.wait_recv()
        self.got = True

    def sent(self):
        if not self.gone:
            self.copy.wait_send()
        self.gone = True


def dot(a, b, dims=(((1,), (0,)), ((), ()))):
    return lax.dot_general(a, b, dims, preferred_element_type=F32)


def kernel(
    lat_in, tgt_in, wgt_in, stu_out, ig_out, g_out,
    kp, km, xs, st, sk, ts, tb, tr, sb, sr, rb, e3, gacc, gb, ga, ra, rs, rd, ysend, yr, zs, zr,
    igp, igr, igc, ia, isum, idr, tgt, wgt, load_sem, send_sem, recv_sem,
):
    dp, row = lax.axis_index("dp"), lax.axis_index("rows")
    k, y, zh = dp % 2, (dp // 2) % 8, dp // 16
    x, zl = row % 4, row // 4

    def dev(dz=0, dy=0, flip=False, dx=0, flip_zl=False):
        core = 1 - k if flip else k
        low = 1 - zl if flip_zl else zl
        return (((zh + dz) % 4 * 8 + (y + dy) % 8) * 2 + core, low * 4 + (x + dx) % 4)

    def row_dev(dr):
        return (dp, (row + dr) % 8)

    copies = []

    def send(src, dst, device):
        i = len(copies)
        copy = pltpu.make_async_remote_copy(
            src_ref=src,
            dst_ref=dst,
            send_sem=send_sem.at[i],
            recv_sem=recv_sem.at[i],
            device_id=device,
            device_id_type=MESH,
        )
        copies.append(Copy(copy))
        return copies[i]

    def blk(dy):
        j = BLOCKS.index(dy % 8)
        return slice(j * 128, j * 128 + 128)

    def rows_of(dx, low):
        at = (zl if low == 0 else 1 - zl) * 4 + (x + dx) % 4
        return pl.ds(pl.multiple_of(at * 80, 16), 80)

    lat = xs.at[0, 32:160]
    loads = []
    for i, (src, dst) in enumerate(((wgt_in, wgt), (lat_in, lat), (tgt_in, tgt))):
        loads.append(pltpu.make_async_copy(src, dst, load_sem.at[i]))
        loads[i].start()

    barrier = pltpu.get_barrier_semaphore()
    partners = [dev(flip_zl=True), dev(dx=1), dev(dx=-1), row_dev(1), row_dev(-1)]
    partners += [dev(dy=dy) for dy in Y_ORDER] + [dev(dz=dz) for dz in (1, 2, 3)]
    partners += [dev(dz=dz, flip=True) for dz in range(4)]
    for partner in partners:
        pl.semaphore_signal(barrier, inc=1, device_id=partner, device_id_type=MESH)

    lane = lax.broadcasted_iota(jnp.int32, (640, 128), 1)
    chan = lax.broadcasted_iota(jnp.int32, (640, 128), 0)
    place = lane + 10 * ((lane * 205) >> 11)
    for s in range(8):
        core = k if s < 4 else 1 - k
        hit = (chan == place + (zh + s % 4) % 4 * 160 + core * 10) & (lane < 80)
        st[:, s * 128 : s * 128 + 128] = jnp.where(hit, 1.0, 0.0).astype(BF16)

    l0 = lax.broadcasted_iota(jnp.int32, (128, 768), 0)
    q = lax.broadcasted_iota(jnp.int32, (128, 768), 1)
    tap = (l0 * 205) >> 11
    third = (tap * 11) >> 5
    want = third * 256 + (tap - 3 * third) * 80 + l0 - 10 * tap
    diff = jnp.where(l0 < 90, q - want, -1)
    for j, dy in enumerate(BLOCKS):
        hit = jnp.where(diff == (y + dy) % 8 * 10, 1.0, 0.0)
        sk[j * 128 : j * 128 + 128, :] = hit.astype(BF16)

    loads[0].wait()
    fill = jnp.zeros((6, 80), F32)
    rows = jnp.concatenate([v for t in range(9) for v in (wgt[t], fill)], axis=0)
    l9 = lax.broadcasted_iota(jnp.int32, (144, 128), 1)
    n9 = lax.broadcasted_iota(jnp.int32, (144, 128), 0)
    pick = (n9 & 15 < 10) & (l9 == (n9 >> 4) * 10 + (n9 & 15))
    pick = jnp.where(pick, 1.0, 0.0).astype(BF16)
    kp[0, 0, :, blk(0)] = dot(rows.astype(BF16), pick, TN).astype(BF16)
    rb[...] = jnp.zeros((1024, 128), BF16)
    loads[2].wait()
    ts[...] = dot(st[...], tgt[...], (((0,), (1,)), ((), ()))).astype(BF16)
    tb[0] = ts[0:80]
    loads[1].wait()
    pl.semaphore_wait(barrier, len(partners))
    p0 = send(kp.at[0, 0, :, blk(0)], kp.at[0, 1, :, blk(0)], dev(flip_zl=True))
    up0 = send(lat.at[0:64], xs.at[3, 32:96], dev(dz=1))
    dn1 = send(lat.at[64:128], xs.at[1, 96:160], dev(dz=-1))
    up1 = send(lat.at[64:128], xs.at[3, 96:160], dev(dz=1))
    dn0 = send(lat.at[0:64], xs.at[1, 32:96], dev(dz=-1))
    part = {0: send(lat, xs.at[4, 32:160], dev(flip=True))}
    top = [send(lat.at[0:32], xs.at[0, 160:192], row_dev(-1))]
    bot = [send(lat.at[96:128], xs.at[0, 0:32], row_dev(1))]

    p0.recv()
    block = kp.at[0, :, :, blk(0)]
    p1, late = {}, {}
    for dy in (2, -2, 1, -1):
        p1[dy] = send(block, kp.at[0, :, :, blk(-dy)], dev(dy=dy))
    right, left, fwd_r, fwd_l = {}, {}, {}, {}
    right[0] = send(block, kp.at[3, :, :, blk(0)], dev(dx=1))
    left[0] = send(block, kp.at[1, :, :, blk(0)], dev(dx=-1))

    halo = {0: (top[0], bot[0])}

    def halos(s):
        up = send(xs.at[s, 32:64], xs.at[s, 160:192], row_dev(-1))
        dn = send(xs.at[s, 128:160], xs.at[s, 0:32], row_dev(1))
        halo[s] = (up, dn)
        part[s] = send(xs.at[s, 32:160], xs.at[s + 4, 32:160], dev(flip=True))

    def x_sends(dy):
        got = kp.at[0, :, :, blk(-dy)]
        right[dy] = send(got, kp.at[3, :, :, blk(-dy)], dev(dx=1))
        left[dy] = send(got, kp.at[1, :, :, blk(-dy)], dev(dx=-1))

    def y_near(dy):
        p1[dy].recv()
        if dy in (2, -2):
            one, half = dy // 2, 0 if dy > 0 else 1
            got = kp.at[0, :, :, blk(-dy)]
            p1[dy + one] = send(got, kp.at[0, :, :, blk(-dy - one)], dev(dy=one))
            dst = kp.at[0, half, :, blk(4)]
            late[half] = send(kp.at[0, half, :, blk(-dy)], dst, dev(dy=dy))
        x_sends(dy)

    def x_step(dy):
        right[dy].recv()
        dst = kp.at[2, 0, :, blk(-dy)]
        fwd_r[dy] = send(kp.at[3, 0, :, blk(-dy)], dst, dev(dx=1))
        left[dy].recv()
        dst = kp.at[2, 1, :, blk(-dy)]
        fwd_l[dy] = send(kp.at[1, 1, :, blk(-dy)], dst, dev(dx=-1))

    def to_group(src_of, dst_of, hops):
        sent = {}
        for s in (4, 1, 3, 5, 7):
            back = s // 4 * 4 + (-s) % 4
            sent[back] = send(src_of(s), dst_of(back), dev(dz=s % 4, flip=s >= 4))
        up = send(src_of(2), hops.at[0], dev(dz=1))
        dn = send(src_of(6), hops.at[1], dev(dz=-1))

        def relay_up():
            up.recv()
            sent[2] = send(hops.at[0], dst_of(2), dev(dz=1))

        def relay_dn():
            dn.recv()
            sent[6] = send(hops.at[1], dst_of(6), dev(dz=-1, flip=True))

        return sent, relay_up, relay_dn

    y_near(2)
    y_near(-2)
    y_near(1)
    y_near(-1)
    x_step(0)
    up0.recv()
    over0 = send(xs.at[3, 32:96], xs.at[2, 32:96], dev(dz=1))
    dn1.recv()
    over1 = send(xs.at[1, 96:160], xs.at[2, 96:160], dev(dz=-1))
    goals, goal_up, goal_dn = to_group(
        lambda s: ts.at[s * 128 : s * 128 + 80], lambda s: tb.at[s], tr
    )
    x_step(2)
    x_step(-2)
    y_near(3)
    y_near(-3)
    late[0].recv()
    late[1].recv()
    x_sends(4)
    x_step(1)
    x_step(-1)
    up1.recv()
    halos(3)
    dn0.recv()
    halos(1)
    x_step(3)
    x_step(-3)
    x_step(4)

    def place_kernel(dx):
        out = dot(kp[dx].reshape(160, 1024), sk[...]).astype(BF16)
        km[rows_of(dx, 0), :] = out[:80]
        km[rows_of(dx, 1), :] = out[80:]

    place_kernel(0)
    place_kernel(1)
    place_kernel(3)

    over0.recv()
    over1.recv()
    halos(2)
    goal_up()
    goal_dn()
    for dy in range(8):
        dy = dy if dy < 5 else dy - 8
        fwd_r[dy].recv()
        fwd_l[dy].recv()
    place_kernel(2)

    col = lax.broadcasted_iota(jnp.int32, (256, 128), 0) % 32
    first, last = col == 0, col == 31
    real = lax.broadcasted_iota(jnp.int32, (256, 128), 1) < 80

    def pair_ready(s):
        ends = []
        for c, edge in zip(halo[s], (slice(160, 192), slice(0, 32))):
            c.recv()
            ends.append(send(xs.at[s, edge], xs.at[s + 4, edge], dev(flip=True)))
        part[s].recv()
        for c in ends:
            c.recv()
            c.sent()

        @pl.when(row == 0)
        def _():
            xs[s, 0:32, :] = jnp.zeros((32, 640), BF16)
            xs[s + 4, 0:32, :] = jnp.zeros((32, 640), BF16)

        @pl.when(row == 7)
        def _():
            xs[s, 160:192, :] = jnp.zeros((32, 640), BF16)
            xs[s + 4, 160:192, :] = jnp.zeros((32, 640), BF16)

        for back in (s, s + 4):
            if back:
                goals[back].recv()

    def joined(ref, s, rows):
        return jnp.concatenate([ref[s, rows], ref[s + 4, rows]], axis=0)

    def forward(s):
        acc = None
        for a in range(3):
            win = joined(xs, s, slice(32 * a, 32 * a + 128))
            term = dot(win, km[:, 256 * a : 256 * a + 256])
            acc = term if acc is None else acc + term
        mid = pltpu.roll(acc, 176, 1)[:, :128]
        end = pltpu.roll(acc, 96, 1)[:, :128]
        total = mid + jnp.where(first, 0.0, pltpu.roll(acc[:, :128], 1, 0))
        total = total + jnp.where(last, 0.0, pltpu.roll(end, 255, 0))
        stu = jnp.where(real, total, 0.0).astype(BF16)
        stu = stu.astype(F32)
        goal = []
        for i, at in enumerate((s, s + 4)):
            sb[at] = stu[128 * i : 128 * i + 128].T[:80].astype(BF16)
            fill = jnp.zeros((48, 128), F32)
            goal.append(jnp.concatenate([tb[at].astype(F32), fill], axis=0).T)
        err = stu - jnp.concatenate(goal, axis=0)
        err = err.astype(BF16).astype(F32)
        zero = jnp.zeros((256, 128), F32)
        nxt = jnp.where(last, 0.0, pltpu.roll(err, 255, 0))
        prv = jnp.where(first, 0.0, pltpu.roll(err, 1, 0))
        wide = jnp.concatenate([nxt, zero], axis=1)
        wide = wide + pltpu.roll(jnp.concatenate([err, zero], axis=1), 80, 1)
        wide = wide + pltpu.roll(jnp.concatenate([prv, zero], axis=1), 160, 1)
        wide = wide.astype(BF16)
        e3[s, 32:160, :] = wide[:128]
        e3[s + 4, 32:160, :] = wide[128:]

    for s in (0, 3, 1, 2):
        pair_ready(s)
        forward(s)

    etop = send(e3.at[:, 32:64], e3.at[:, 160:192], row_dev(-1))
    ebot = send(e3.at[:, 128:160], e3.at[:, 0:32], row_dev(1))
    stus, stu_up, stu_dn = to_group(
        lambda s: sb.at[s], lambda s: rb.at[s * 128 : s * 128 + 80], sr
    )
    rb[0:80] = sb[0]

    gacc[...] = jnp.zeros((640, 768), F32)

    def weight_grad(m, carry):
        two = pl.ds(2 * m, 2)
        errs = e3[two, 32:160, :].reshape(256, 256)
        for a in range(3):
            win = xs[two, 32 * a : 32 * a + 128, :].reshape(256, 640)
            gacc[:, 256 * a : 256 * a + 256] += dot(win, errs, TN)
        return carry

    lax.fori_loop(0, 4, weight_grad, 0)
    gb[...] = gacc[...].astype(BF16)

    first_hop, raw, second_hop = [], [], []

    def place_grad(g):
        cols = slice(*GROUPS[g])
        ga[:, cols] = dot(gb[...], sk[cols, :], NT).astype(BF16)
        up = send(ga.at[rows_of(2, 0), cols], ra.at[0, :, cols], dev(dx=1))
        dn = send(ga.at[rows_of(2, 1), cols], ra.at[1, :, cols], dev(dx=-1))
        first_hop.append((up, dn))
        up = send(ga.at[rows_of(1, 1), cols], rd.at[1, :, cols], dev(dx=1))
        dn = send(ga.at[rows_of(3, 0), cols], rd.at[0, :, cols], dev(dx=-1))
        raw.append((up, dn))

    def relay(g):
        cols = slice(*GROUPS[g])
        up, dn = first_hop[g]
        up.recv()
        rs[0, :, cols] = (ra[0, :, cols].astype(F32) + ga[rows_of(1, 0), cols].astype(F32)).astype(BF16)
        up = send(rs.at[0, :, cols], rd.at[2, :, cols], dev(dx=1))
        dn.recv()
        rs[1, :, cols] = (ra[1, :, cols].astype(F32) + ga[rows_of(3, 1), cols].astype(F32)).astype(BF16)
        dn = send(rs.at[1, :, cols], rd.at[3, :, cols], dev(dx=-1))
        second_hop.append((up, dn))

    ysent = []

    def spread(g):
        cols = slice(*GROUPS[g])
        for c in raw[g] + second_hop[g]:
            c.recv()
        for i in range(2):
            mine = ga[rows_of(0, i), cols].astype(F32)
            both = rd[i, :, cols].astype(F32) + rd[i + 2, :, cols].astype(F32)
            ysend[i, :, cols] = (mine + both).astype(BF16)
        for dy in BLOCKS[GROUPS[g][0] // 128 : GROUPS[g][1] // 128]:
            if dy:
                ysent.append(send(ysend.at[:, :, blk(dy)], yr.at[len(ysent)], dev(dy=dy)))

    place_grad(0)
    etop.recv()
    ebot.recv()
    etop.sent()
    ebot.sent()

    @pl.when(row == 0)
    def _():
        e3[:, 0:32, :] = jnp.zeros((8, 32, 256), BF16)

    @pl.when(row == 7)
    def _():
        e3[:, 160:192, :] = jnp.zeros((8, 32, 256), BF16)

    ip = {}

    def input_grad(s):
        acc = None
        for a in range(3):
            win = e3[s : s + 2, 64 - 32 * a : 192 - 32 * a, :].reshape(256, 256)
            term = dot(win, km[:, 256 * a : 256 * a + 256], NT)
            acc = term if acc is None else acc + term
        igp[s : s + 2] = acc.astype(BF16).reshape(2, 128, 640)
        if s >= 4:
            ip[s - 4] = send(igp.at[s : s + 2], igr.at[s - 4 : s - 2], dev(flip=True))

    def core_sum(s):
        igc[s] = (igp[s].astype(F32) + igr[s].astype(F32)).astype(BF16)

    input_grad(6)
    input_grad(2)
    place_grad(1)
    ip[2].recv()
    core_sum(2)
    ir_a = send(igc.at[2, 0:64], ia.at[0], dev(dz=1))
    ir_b = send(igc.at[2, 64:128], ia.at[1], dev(dz=-1))
    core_sum(3)
    id_b = send(igc.at[3, 0:64], idr.at[0], dev(dz=-1))
    place_grad(2)
    input_grad(4)
    input_grad(0)
    stu_up()
    stu_dn()
    relay(0)
    ip[0].recv()
    core_sum(1)
    id_a = send(igc.at[1, 64:128], idr.at[1], dev(dz=1))
    core_sum(0)
    relay(1)
    relay(2)
    spread(0)

    ir_a.recv()
    isum[0] = (ia[0].astype(F32) + igc[1, 0:64].astype(F32)).astype(BF16)
    is_a = send(isum.at[0], idr.at[2], dev(dz=1))
    ir_b.recv()
    isum[1] = (ia[1].astype(F32) + igc[3, 64:128].astype(F32)).astype(BF16)
    is_b = send(isum.at[1], idr.at[3], dev(dz=-1))

    spread(1)
    spread(2)
    for c in stus.values():
        c.recv()
    stu_out[...] = dot(rb[...], st[...], (((0,), (1,)), ((), ()))).astype(BF16)

    total = ysend[:, :, blk(0)].astype(F32)
    for i in range(7):
        ysent[i].recv()
        total = total + yr[i].astype(F32)
    zs[...] = total
    zc = send(zs.at[1], zr, dev(flip_zl=True))

    for c in (id_a, id_b, is_a, is_b):
        c.recv()
    low = igc[0, 0:64].astype(F32) + idr[0].astype(F32) + idr[2].astype(F32)
    high = igc[0, 64:128].astype(F32) + idr[1].astype(F32) + idr[3].astype(F32)
    ig_out[0:64] = low.astype(BF16)
    ig_out[64:128] = high.astype(BF16)

    zc.recv()
    grad = (zs[0] + zr[...]) * (1.0 / 64.0)
    turned = jnp.concatenate([grad, jnp.zeros((48, 128), F32)], axis=0).T
    for t in range(9):
        g_out[t] = turned[10 * t : 10 * t + 10, :80]
    for c in copies:
        c.sent()


def per_device(latents, target, weight, moment1, moment2):
    vmem = pl.BlockSpec(memory_space=pltpu.VMEM)
    student, input_grad, grad = pl.pallas_call(
        kernel,
        out_shape=(
            jax.ShapeDtypeStruct((128, 640), BF16),
            jax.ShapeDtypeStruct((128, 640), BF16),
            jax.ShapeDtypeStruct((9, 10, 80), F32),
        ),
        in_specs=[pl.BlockSpec(memory_space=pl.ANY)] * 3,
        out_specs=(vmem,) * 3,
        scratch_shapes=[
            pltpu.VMEM((4, 2, 80, 1024), BF16),
            pltpu.VMEM((640, 768), BF16),
            pltpu.VMEM((8, 192, 640), BF16),
            pltpu.VMEM((640, 1024), BF16),
            pltpu.VMEM((1024, 768), BF16),
            pltpu.VMEM((1024, 128), BF16),
            pltpu.VMEM((8, 80, 128), BF16),
            pltpu.VMEM((2, 80, 128), BF16),
            pltpu.VMEM((8, 80, 128), BF16),
            pltpu.VMEM((2, 80, 128), BF16),
            pltpu.VMEM((1024, 128), BF16),
            pltpu.VMEM((8, 192, 256), BF16),
            pltpu.VMEM((640, 768), F32),
            pltpu.VMEM((640, 768), BF16),
            pltpu.VMEM((640, 1024), BF16),
            pltpu.VMEM((2, 80, 1024), BF16),
            pltpu.VMEM((2, 80, 1024), BF16),
            pltpu.VMEM((4, 80, 1024), BF16),
            pltpu.VMEM((2, 80, 1024), BF16),
            pltpu.VMEM((7, 2, 80, 128), BF16),
            pltpu.VMEM((2, 80, 128), F32),
            pltpu.VMEM((80, 128), F32),
            pltpu.VMEM((8, 128, 640), BF16),
            pltpu.VMEM((4, 128, 640), BF16),
            pltpu.VMEM((4, 128, 640), BF16),
            pltpu.VMEM((2, 64, 640), BF16),
            pltpu.VMEM((2, 64, 640), BF16),
            pltpu.VMEM((4, 64, 640), BF16),
            pltpu.VMEM((128, 640), BF16),
            pltpu.VMEM((9, 10, 80), F32),
            pltpu.SemaphoreType.DMA((3,)),
            pltpu.SemaphoreType.DMA((N_SEM,)),
            pltpu.SemaphoreType.DMA((N_SEM,)),
        ],
        compiler_params=pltpu.CompilerParams(
            collective_id=0, has_side_effects=True, vmem_limit_bytes=60600 << 10
        ),
    )(latents.reshape(128, 640), target.reshape(128, 640), weight.transpose(0, 2, 1))
    grad = grad.transpose(0, 2, 1)
    new_moment1 = 0.9 * moment1 + 0.1 * grad
    new_moment2 = 0.999 * moment2 + 0.001 * grad * grad
    new_weight = weight - 0.01 * new_moment1 / (jnp.sqrt(new_moment2) + 1e-08)
    return (
        student.reshape(latents.shape),
        input_grad.reshape(latents.shape),
        new_weight,
        new_moment1,
        new_moment2,
    )


def solution(mesh):
    act = P("dp", "rows", None, None)
    par = P(None, "rows", "dp")
    return jax.shard_map(
        per_device,
        mesh=mesh,
        in_specs=(act, act, par, par, par),
        out_specs=(act, act, par, par, par),
        check_vma=False,
    )
```

```python
import jax
import jax.numpy as jnp
from jax import lax
from jax.experimental import pallas as pl
from jax.experimental.pallas import tpu as pltpu
from jax.sharding import PartitionSpec as P

MESH = pl.DeviceIdType.MESH
F32 = jnp.float32
BF16 = jnp.bfloat16
Y_ORDER = (1, 7, 2, 6, 3, 5, 4)
BLOCKS = (4, 3, 5, 2, 6, 1, 7, 0)
GROUPS = ((0, 384), (384, 640), (640, 1024))
N_SEM = 125
NT = (((1,), (1,)), ((), ()))
TN = (((0,), (0,)), ((), ()))


class Copy:
    def __init__(self, copy):
        self.copy, self.got, self.gone = copy, False, False
        copy.start()

    def recv(self):
        if not self.got:
            self.copy.wait_recv()
        self.got = True

    def sent(self):
        if not self.gone:
            self.copy.wait_send()
        self.gone = True


def dot(a, b, dims=(((1,), (0,)), ((), ()))):
    return lax.dot_general(a, b, dims, preferred_element_type=F32)


def kernel(
    lat_in, tgt_in, wgt_in, stu_out, ig_out, g_out,
    kp, km, xs, st, sk, ts, tb, tr, sb, sr, rb, eb, hb, e3, gacc, gb, ga, ra, rs, rd, ysend, yr, zs, zr,
    igp, igr, igc, ia, isum, idr, tgt, wgt, load_sem, send_sem, recv_sem,
):
    dp, row = lax.axis_index("dp"), lax.axis_index("rows")
    k, y, zh = dp % 2, (dp // 2) % 8, dp // 16
    x, zl = row % 4, row // 4

    def dev(dz=0, dy=0, flip=False, dx=0, flip_zl=False):
        core = 1 - k if flip else k
        low = 1 - zl if flip_zl else zl
        return (((zh + dz) % 4 * 8 + (y + dy) % 8) * 2 + core, low * 4 + (x + dx) % 4)

    def row_dev(dr):
        return (dp, (row + dr) % 8)

    copies = []

    def send(src, dst, device):
        i = len(copies)
        copy = pltpu.make_async_remote_copy(
            src_ref=src,
            dst_ref=dst,
            send_sem=send_sem.at[i],
            recv_sem=recv_sem.at[i],
            device_id=device,
            device_id_type=MESH,
        )
        copies.append(Copy(copy))
        return copies[i]

    def blk(dy):
        j = BLOCKS.index(dy % 8)
        return slice(j * 128, j * 128 + 128)

    def rows_of(dx, low):
        at = (zl if low == 0 else 1 - zl) * 4 + (x + dx) % 4
        return pl.ds(pl.multiple_of(at * 80, 16), 80)

    lat = xs.at[0, 32:160]
    loads = []
    for i, (src, dst) in enumerate(((wgt_in, wgt), (lat_in, lat), (tgt_in, tgt))):
        loads.append(pltpu.make_async_copy(src, dst, load_sem.at[i]))
        loads[i].start()

    barrier = pltpu.get_barrier_semaphore()
    partners = [dev(flip_zl=True), dev(dx=1), dev(dx=-1), row_dev(1), row_dev(-1)]
    partners += [dev(dy=dy) for dy in Y_ORDER] + [dev(dz=dz) for dz in (1, 2, 3)]
    partners += [dev(dz=dz, flip=True) for dz in range(4)]
    partners += [dev(dy=dy, flip_zl=True) for dy in (1, -1, 2, -2)]
    for partner in partners:
        pl.semaphore_signal(barrier, inc=1, device_id=partner, device_id_type=MESH)

    loads[0].wait()
    fill = jnp.zeros((6, 80), F32)
    rows = jnp.concatenate([v for t in range(9) for v in (wgt[t], fill)], axis=0)
    l9 = lax.broadcasted_iota(jnp.int32, (144, 128), 1)
    n9 = lax.broadcasted_iota(jnp.int32, (144, 128), 0)
    pick = (n9 & 15 < 10) & (l9 == (n9 >> 4) * 10 + (n9 & 15))
    pick = jnp.where(pick, 1.0, 0.0).astype(BF16)
    kp[0, 0, :, blk(0)] = dot(rows.astype(BF16), pick, TN).astype(BF16)
    rb[...] = jnp.zeros((1024, 128), BF16)
    loads[1].wait()
    pl.semaphore_wait(barrier, len(partners))
    p1, late = {}, {}
    own = kp.at[0, 0, :, blk(0)]
    for dy in (2, -2, 1, -1, 0):
        for i in (1, 0) if dy else (1,):
            p1[dy, i] = send(own, kp.at[0, i, :, blk(-dy)], dev(dy=dy, flip_zl=i == 1))
    top = [send(lat.at[0:32], xs.at[0, 160:192], row_dev(-1))]
    bot = [send(lat.at[96:128], xs.at[0, 0:32], row_dev(1))]
    up0 = send(lat.at[0:64], xs.at[3, 32:96], dev(dz=1))
    dn1 = send(lat.at[64:128], xs.at[1, 96:160], dev(dz=-1))
    up1 = send(lat.at[64:128], xs.at[3, 96:160], dev(dz=1))
    dn0 = send(lat.at[0:64], xs.at[1, 32:96], dev(dz=-1))
    part = {0: send(lat, xs.at[4, 32:160], dev(flip=True))}

    lane = lax.broadcasted_iota(jnp.int32, (640, 128), 1)
    chan = lax.broadcasted_iota(jnp.int32, (640, 128), 0)
    place = lane + 10 * ((lane * 205) >> 11)
    for s in range(8):
        core = k if s < 4 else 1 - k
        hit = (chan == place + (zh + s % 4) % 4 * 160 + core * 10) & (lane < 80)
        st[:, s * 128 : s * 128 + 128] = jnp.where(hit, 1.0, 0.0).astype(BF16)

    l0 = lax.broadcasted_iota(jnp.int32, (128, 768), 0)
    q = lax.broadcasted_iota(jnp.int32, (128, 768), 1)
    tap = (l0 * 205) >> 11
    third = (tap * 11) >> 5
    want = third * 256 + (tap - 3 * third) * 80 + l0 - 10 * tap
    diff = jnp.where(l0 < 90, q - want, -1)
    for j, dy in enumerate(BLOCKS):
        hit = jnp.where(diff == (y + dy) % 8 * 10, 1.0, 0.0)
        sk[j * 128 : j * 128 + 128, :] = hit.astype(BF16)

    loads[2].wait()
    ts[...] = dot(st[...], tgt[...], (((0,), (1,)), ((), ()))).astype(BF16)
    tb[0] = ts[0:80]
    right, left, fwd_r, fwd_l = {}, {}, {}, {}

    halo = {0: (top[0], bot[0])}

    def halos(s):
        up = send(xs.at[s, 32:64], xs.at[s, 160:192], row_dev(-1))
        dn = send(xs.at[s, 128:160], xs.at[s, 0:32], row_dev(1))
        halo[s] = (up, dn)
        part[s] = send(xs.at[s, 32:160], xs.at[s + 4, 32:160], dev(flip=True))

    def x_sends(dy):
        got = kp.at[0, :, :, blk(-dy)]
        right[dy] = send(got, kp.at[3, :, :, blk(-dy)], dev(dx=1))
        left[dy] = send(got, kp.at[1, :, :, blk(-dy)], dev(dx=-1))

    def y_near(dy):
        p1[dy, 1].recv()
        p1[dy, 0].recv()
        if dy in (2, -2):
            one, half = dy // 2, 0 if dy > 0 else 1
            dst = kp.at[0, half, :, blk(4)]
            late[half] = send(kp.at[0, half, :, blk(-dy)], dst, dev(dy=dy))
            got = kp.at[0, :, :, blk(-dy)]
            late[dy + one] = send(got, kp.at[0, :, :, blk(-dy - one)], dev(dy=one))
        x_sends(dy)

    ends = {}

    def edges(s):
        ends[s] = []
        for c, edge in zip(halo[s], (slice(160, 192), slice(0, 32))):
            c.recv()
            ends[s].append(send(xs.at[s, edge], xs.at[s + 4, edge], dev(flip=True)))

    def x_step(dy):
        right[dy].recv()
        dst = kp.at[2, 0, :, blk(-dy)]
        fwd_r[dy] = send(kp.at[3, 0, :, blk(-dy)], dst, dev(dx=1))
        left[dy].recv()
        dst = kp.at[2, 1, :, blk(-dy)]
        fwd_l[dy] = send(kp.at[1, 1, :, blk(-dy)], dst, dev(dx=-1))

    def to_group(src_of, dst_of, hops):
        sent = {}
        for s in (4, 1, 3, 5, 7):
            back = s // 4 * 4 + (-s) % 4
            sent[back] = send(src_of(s), dst_of(back), dev(dz=s % 4, flip=s >= 4))
        up = send(src_of(2), hops.at[0], dev(dz=1))
        dn = send(src_of(6), hops.at[1], dev(dz=-1))

        def relay_up():
            up.recv()
            sent[2] = send(hops.at[0], dst_of(2), dev(dz=1))

        def relay_dn():
            dn.recv()
            sent[6] = send(hops.at[1], dst_of(6), dev(dz=-1, flip=True))

        return sent, relay_up, relay_dn

    p1[0, 1].recv()
    x_sends(0)
    y_near(2)
    y_near(-2)
    y_near(1)
    y_near(-1)
    x_step(0)
    up0.recv()
    over0 = send(xs.at[3, 32:96], xs.at[2, 32:96], dev(dz=1))
    dn1.recv()
    over1 = send(xs.at[1, 96:160], xs.at[2, 96:160], dev(dz=-1))
    x_step(2)
    x_step(-2)
    for dy in (3, -3):
        late[dy].recv()
        x_sends(dy)
    late[0].recv()
    late[1].recv()
    x_sends(4)
    x_step(1)
    x_step(-1)
    up1.recv()
    halos(3)
    dn0.recv()
    halos(1)
    goals, goal_up, goal_dn = to_group(
        lambda s: ts.at[s * 128 : s * 128 + 80], lambda s: tb.at[s], tr
    )
    x_step(3)
    x_step(-3)
    over0.recv()
    over1.recv()
    halos(2)
    x_step(4)
    edges(0)
    edges(3)
    edges(1)

    def place_kernel(dx):
        out = dot(kp[dx].reshape(160, 1024), sk[...]).astype(BF16)
        km[rows_of(dx, 0), :] = out[:80]
        km[rows_of(dx, 1), :] = out[80:]

    place_kernel(0)
    edges(2)
    goal_up()
    goal_dn()
    place_kernel(1)
    place_kernel(3)

    for dy in range(8):
        dy = dy if dy < 5 else dy - 8
        fwd_r[dy].recv()
        fwd_l[dy].recv()
    place_kernel(2)

    col = lax.broadcasted_iota(jnp.int32, (256, 128), 0) % 32
    first, last = col == 0, col == 31
    real = lax.broadcasted_iota(jnp.int32, (256, 128), 1) < 80

    def pair_ready(s):
        part[s].recv()
        for c in ends[s]:
            c.recv()
            c.sent()

        @pl.when(row == 0)
        def _():
            xs[s, 0:32, :] = jnp.zeros((32, 640), BF16)
            xs[s + 4, 0:32, :] = jnp.zeros((32, 640), BF16)

        @pl.when(row == 7)
        def _():
            xs[s, 160:192, :] = jnp.zeros((32, 640), BF16)
            xs[s + 4, 160:192, :] = jnp.zeros((32, 640), BF16)

        for back in (s, s + 4):
            if back:
                goals[back].recv()

    def joined(ref, s, rows):
        return jnp.concatenate([ref[s, rows], ref[s + 4, rows]], axis=0)

    def widened(err):
        zero = jnp.zeros((256, 128), F32)
        nxt = jnp.where(last, 0.0, pltpu.roll(err, 255, 0))
        prv = jnp.where(first, 0.0, pltpu.roll(err, 1, 0))
        wide = jnp.concatenate([nxt, zero], axis=1)
        wide = wide + pltpu.roll(jnp.concatenate([err, zero], axis=1), 80, 1)
        wide = wide + pltpu.roll(jnp.concatenate([prv, zero], axis=1), 160, 1)
        return wide.astype(BF16)

    def forward(s):
        acc = None
        for a in range(3):
            win = joined(xs, s, slice(32 * a, 32 * a + 128))
            term = dot(win, km[:, 256 * a : 256 * a + 256])
            acc = term if acc is None else acc + term
        mid = pltpu.roll(acc, 176, 1)[:, :128]
        end = pltpu.roll(acc, 96, 1)[:, :128]
        total = mid + jnp.where(first, 0.0, pltpu.roll(acc[:, :128], 1, 0))
        total = total + jnp.where(last, 0.0, pltpu.roll(end, 255, 0))
        stu = jnp.where(real, total, 0.0).astype(BF16)
        stu = stu.astype(F32)
        goal = []
        for i, at in enumerate((s, s + 4)):
            sb[at] = stu[128 * i : 128 * i + 128].T[:80].astype(BF16)
            fill = jnp.zeros((48, 128), F32)
            goal.append(jnp.concatenate([tb[at].astype(F32), fill], axis=0).T)
        err = stu - jnp.concatenate(goal, axis=0)
        err = err.astype(BF16).astype(F32)
        for i, at in enumerate((s, s + 4)):
            eb[at] = err[128 * i : 128 * i + 128].astype(BF16)
        wide = widened(err)
        e3[s, 32:160, :] = wide[:128]
        e3[s + 4, 32:160, :] = wide[128:]

    err_halos = []
    for s in (0, 3, 1, 2):
        pair_ready(s)
        forward(s)
    err_halos.append(send(eb.at[:, 0:32], hb.at[1], row_dev(-1)))
    err_halos.append(send(eb.at[:, 96:128], hb.at[0], row_dev(1)))
    stus, stu_up, stu_dn = to_group(
        lambda s: sb.at[s], lambda s: rb.at[s * 128 : s * 128 + 80], sr
    )
    rb[0:80] = sb[0]

    gacc[...] = jnp.zeros((640, 768), F32)

    def weight_grad(m, carry):
        two = pl.ds(2 * m, 2)
        errs = e3[two, 32:160, :].reshape(256, 256)
        for a in range(3):
            win = xs[two, 32 * a : 32 * a + 128, :].reshape(256, 640)
            gacc[:, 256 * a : 256 * a + 256] += dot(win, errs, TN)
        return carry

    lax.fori_loop(0, 4, weight_grad, 0)
    gb[...] = gacc[...].astype(BF16)

    first_hop, raw, second_hop = [], [], []

    def place_grad(g):
        cols = slice(*GROUPS[g])
        ga[:, cols] = dot(gb[...], sk[cols, :], NT).astype(BF16)
        up = send(ga.at[rows_of(2, 0), cols], ra.at[0, :, cols], dev(dx=1))
        dn = send(ga.at[rows_of(2, 1), cols], ra.at[1, :, cols], dev(dx=-1))
        first_hop.append((up, dn))
        up = send(ga.at[rows_of(1, 1), cols], rd.at[1, :, cols], dev(dx=1))
        dn = send(ga.at[rows_of(3, 0), cols], rd.at[0, :, cols], dev(dx=-1))
        raw.append((up, dn))

    def relay(g):
        cols = slice(*GROUPS[g])
        up, dn = first_hop[g]
        up.recv()
        rs[0, :, cols] = (ra[0, :, cols].astype(F32) + ga[rows_of(1, 0), cols].astype(F32)).astype(BF16)
        up = send(rs.at[0, :, cols], rd.at[2, :, cols], dev(dx=1))
        dn.recv()
        rs[1, :, cols] = (ra[1, :, cols].astype(F32) + ga[rows_of(3, 1), cols].astype(F32)).astype(BF16)
        dn = send(rs.at[1, :, cols], rd.at[3, :, cols], dev(dx=-1))
        second_hop.append((up, dn))

    ysent = []

    def spread(g):
        cols = slice(*GROUPS[g])
        for c in raw[g] + second_hop[g]:
            c.recv()
        for i in range(2):
            mine = ga[rows_of(0, i), cols].astype(F32)
            both = rd[i, :, cols].astype(F32) + rd[i + 2, :, cols].astype(F32)
            ysend[i, :, cols] = (mine + both).astype(BF16)
        for dy in BLOCKS[cols.start // 128 : cols.stop // 128]:
            if dy:
                ysent.append(send(ysend.at[:, :, blk(dy)], yr.at[len(ysent)], dev(dy=dy)))

    place_grad(0)
    place_grad(1)
    place_grad(2)
    for c in err_halos:
        c.recv()
    for i, edge in enumerate((slice(0, 32), slice(160, 192))):
        wide = widened(hb[i].reshape(256, 128).astype(F32))
        e3[:, edge, :] = wide.reshape(8, 32, 256)

    @pl.when(row == 0)
    def _():
        e3[:, 0:32, :] = jnp.zeros((8, 32, 256), BF16)

    @pl.when(row == 7)
    def _():
        e3[:, 160:192, :] = jnp.zeros((8, 32, 256), BF16)

    ip = {}

    def input_grad(s):
        acc = None
        for a in range(3):
            win = e3[s : s + 2, 64 - 32 * a : 192 - 32 * a, :].reshape(256, 256)
            term = dot(win, km[:, 256 * a : 256 * a + 256], NT)
            acc = term if acc is None else acc + term
        igp[s : s + 2] = acc.astype(BF16).reshape(2, 128, 640)
        if s >= 4:
            ip[s - 4] = send(igp.at[s : s + 2], igr.at[s - 4 : s - 2], dev(flip=True))

    def core_sum(s):
        igc[s] = (igp[s].astype(F32) + igr[s].astype(F32)).astype(BF16)

    input_grad(6)
    input_grad(2)
    ip[2].recv()
    core_sum(2)
    ir_a = send(igc.at[2, 0:64], ia.at[0], dev(dz=1))
    ir_b = send(igc.at[2, 64:128], ia.at[1], dev(dz=-1))
    core_sum(3)
    id_b = send(igc.at[3, 0:64], idr.at[0], dev(dz=-1))
    stu_up()
    stu_dn()
    input_grad(4)
    relay(0)
    input_grad(0)
    ip[0].recv()
    core_sum(1)
    id_a = send(igc.at[1, 64:128], idr.at[1], dev(dz=1))
    core_sum(0)
    relay(1)
    relay(2)
    spread(0)
    spread(1)

    ir_a.recv()
    isum[0] = (ia[0].astype(F32) + igc[1, 0:64].astype(F32)).astype(BF16)
    is_a = send(isum.at[0], idr.at[2], dev(dz=1))
    ir_b.recv()
    isum[1] = (ia[1].astype(F32) + igc[3, 64:128].astype(F32)).astype(BF16)
    is_b = send(isum.at[1], idr.at[3], dev(dz=-1))

    spread(2)
    total = ysend[:, :, blk(0)].astype(F32)
    for i in range(7):
        ysent[i].recv()
        total = total + yr[i].astype(F32)
    zs[...] = total
    zc = send(zs.at[1], zr, dev(flip_zl=True))
    for c in stus.values():
        c.recv()
    stu_out[...] = dot(rb[...], st[...], (((0,), (1,)), ((), ()))).astype(BF16)


    for c in (id_a, id_b, is_a, is_b):
        c.recv()
    low = igc[0, 0:64].astype(F32) + idr[0].astype(F32) + idr[2].astype(F32)
    high = igc[0, 64:128].astype(F32) + idr[1].astype(F32) + idr[3].astype(F32)
    ig_out[0:64] = low.astype(BF16)
    ig_out[64:128] = high.astype(BF16)

    zc.recv()
    total = zs[0] + zr[...]
    grad = total * (1.0 / 64.0)
    turned = jnp.concatenate([grad, jnp.zeros((48, 128), F32)], axis=0).T
    for t in range(9):
        g_out[t] = turned[10 * t : 10 * t + 10, :80]
    for c in copies:
        c.sent()


def per_device(latents, target, weight, moment1, moment2):
    vmem = pl.BlockSpec(memory_space=pltpu.VMEM)
    student, input_grad, grad = pl.pallas_call(
        kernel,
        out_shape=(
            jax.ShapeDtypeStruct((128, 640), BF16),
            jax.ShapeDtypeStruct((128, 640), BF16),
            jax.ShapeDtypeStruct((9, 10, 80), F32),
        ),
        in_specs=[pl.BlockSpec(memory_space=pl.ANY)] * 3,
        out_specs=(vmem,) * 3,
        scratch_shapes=[
            pltpu.VMEM((4, 2, 80, 1024), BF16),
            pltpu.VMEM((640, 768), BF16),
            pltpu.VMEM((8, 192, 640), BF16),
            pltpu.VMEM((640, 1024), BF16),
            pltpu.VMEM((1024, 768), BF16),
            pltpu.VMEM((1024, 128), BF16),
            pltpu.VMEM((8, 80, 128), BF16),
            pltpu.VMEM((2, 80, 128), BF16),
            pltpu.VMEM((8, 80, 128), BF16),
            pltpu.VMEM((2, 80, 128), BF16),
            pltpu.VMEM((1024, 128), BF16),
            pltpu.VMEM((8, 128, 128), BF16),
            pltpu.VMEM((2, 8, 32, 128), BF16),
            pltpu.VMEM((8, 192, 256), BF16),
            pltpu.VMEM((640, 768), F32),
            pltpu.VMEM((640, 768), BF16),
            pltpu.VMEM((640, 1024), BF16),
            pltpu.VMEM((2, 80, 1024), BF16),
            pltpu.VMEM((2, 80, 1024), BF16),
            pltpu.VMEM((4, 80, 1024), BF16),
            pltpu.VMEM((2, 80, 1024), BF16),
            pltpu.VMEM((7, 2, 80, 128), BF16),
            pltpu.VMEM((2, 80, 128), F32),
            pltpu.VMEM((80, 128), F32),
            pltpu.VMEM((8, 128, 640), BF16),
            pltpu.VMEM((4, 128, 640), BF16),
            pltpu.VMEM((4, 128, 640), BF16),
            pltpu.VMEM((2, 64, 640), BF16),
            pltpu.VMEM((2, 64, 640), BF16),
            pltpu.VMEM((4, 64, 640), BF16),
            pltpu.VMEM((128, 640), BF16),
            pltpu.VMEM((9, 10, 80), F32),
            pltpu.SemaphoreType.DMA((3,)),
            pltpu.SemaphoreType.DMA((N_SEM,)),
            pltpu.SemaphoreType.DMA((N_SEM,)),
        ],
        compiler_params=pltpu.CompilerParams(
            collective_id=0, has_side_effects=True, vmem_limit_bytes=48 << 20
        ),
    )(latents.reshape(128, 640), target.reshape(128, 640), weight.transpose(0, 2, 1))
    grad = grad.transpose(0, 2, 1)
    new_moment1 = 0.9 * moment1 + 0.1 * grad
    new_moment2 = 0.999 * moment2 + 0.001 * grad * grad
    new_weight = weight - 0.01 * new_moment1 / (jnp.sqrt(new_moment2) + 1e-08)
    return (
        student.reshape(latents.shape),
        input_grad.reshape(latents.shape),
        new_weight,
        new_moment1,
        new_moment2,
    )


def solution(mesh):
    act = P("dp", "rows", None, None)
    par = P(None, "rows", "dp")
    return jax.shard_map(
        per_device,
        mesh=mesh,
        in_specs=(act, act, par, par, par),
        out_specs=(act, act, par, par, par),
        check_vma=False,
    )
```

```python
import jax
import jax.numpy as jnp
from jax import lax
from jax.experimental import pallas as pl
from jax.experimental.pallas import tpu as pltpu
from jax.sharding import PartitionSpec as P

MESH = pl.DeviceIdType.MESH
F32 = jnp.float32
BF16 = jnp.bfloat16
Y_ORDER = (1, 7, 2, 6, 3, 5, 4)
BLOCKS = (4, 3, 5, 2, 6, 1, 7, 0)
GROUPS = ((0, 384), (384, 640), (640, 1024))
N_SEM = 125
NT = (((1,), (1,)), ((), ()))
TN = (((0,), (0,)), ((), ()))


class Copy:
    def __init__(self, copy):
        self.copy, self.got, self.gone = copy, False, False
        copy.start()

    def recv(self):
        if not self.got:
            self.copy.wait_recv()
        self.got = True

    def sent(self):
        if not self.gone:
            self.copy.wait_send()
        self.gone = True


def dot(a, b, dims=(((1,), (0,)), ((), ()))):
    return lax.dot_general(a, b, dims, preferred_element_type=F32)


def kernel(
    lat_in, tgt_in, wgt_in, stu_out, ig_out, g_out,
    kp, km, xs, st, sk, ts, tb, tr, sn, sb, sr, rb, eb, hb, e3, gacc, gb, ga, ra, rs, rd, ysend, yr, zs, zr,
    igp, igr, igc, ia, isum, idr, tgt, wgt, load_sem, send_sem, recv_sem,
):
    dp, row = lax.axis_index("dp"), lax.axis_index("rows")
    k, y, zh = dp % 2, (dp // 2) % 8, dp // 16
    x, zl = row % 4, row // 4

    def dev(dz=0, dy=0, flip=False, dx=0, flip_zl=False):
        core = 1 - k if flip else k
        low = 1 - zl if flip_zl else zl
        return (((zh + dz) % 4 * 8 + (y + dy) % 8) * 2 + core, low * 4 + (x + dx) % 4)

    def row_dev(dr):
        return (dp, (row + dr) % 8)

    copies = []

    def send(src, dst, device):
        i = len(copies)
        copy = pltpu.make_async_remote_copy(
            src_ref=src,
            dst_ref=dst,
            send_sem=send_sem.at[i],
            recv_sem=recv_sem.at[i],
            device_id=device,
            device_id_type=MESH,
        )
        copies.append(Copy(copy))
        return copies[i]

    def blk(dy):
        j = BLOCKS.index(dy % 8)
        return slice(j * 128, j * 128 + 128)

    def rows_of(dx, low):
        at = (zl if low == 0 else 1 - zl) * 4 + (x + dx) % 4
        return pl.ds(pl.multiple_of(at * 80, 16), 80)

    lat = xs.at[0, 32:160]
    loads = []
    for i, (src, dst) in enumerate(((wgt_in, wgt), (lat_in, lat), (tgt_in, tgt))):
        loads.append(pltpu.make_async_copy(src, dst, load_sem.at[i]))
        loads[i].start()

    barrier = pltpu.get_barrier_semaphore()
    partners = [dev(flip_zl=True), dev(dx=1), dev(dx=-1), row_dev(1), row_dev(-1)]
    partners += [dev(dy=dy) for dy in Y_ORDER] + [dev(dz=dz) for dz in (1, 2, 3)]
    partners += [dev(dz=dz, flip=True) for dz in range(4)]
    partners += [dev(dy=dy, flip_zl=True) for dy in (1, -1, 2, -2)]
    for partner in partners:
        pl.semaphore_signal(barrier, inc=1, device_id=partner, device_id_type=MESH)

    loads[0].wait()
    fill = jnp.zeros((6, 80), F32)
    rows = jnp.concatenate([v for t in range(9) for v in (wgt[t], fill)], axis=0)
    l9 = lax.broadcasted_iota(jnp.int32, (144, 128), 1)
    n9 = lax.broadcasted_iota(jnp.int32, (144, 128), 0)
    pick = (n9 & 15 < 10) & (l9 == (n9 >> 4) * 10 + (n9 & 15))
    pick = jnp.where(pick, 1.0, 0.0).astype(BF16)
    kp[0, 0, :, blk(0)] = dot(rows.astype(BF16), pick, TN).astype(BF16)
    rb[...] = jnp.zeros((1024, 128), BF16)
    loads[1].wait()
    pl.semaphore_wait(barrier, len(partners))
    p1, late = {}, {}
    own = kp.at[0, 0, :, blk(0)]
    for dy in (2, -2, 1, -1, 0):
        for i in (1, 0) if dy else (1,):
            p1[dy, i] = send(own, kp.at[0, i, :, blk(-dy)], dev(dy=dy, flip_zl=i == 1))
    top = [send(lat.at[0:32], xs.at[0, 160:192], row_dev(-1))]
    bot = [send(lat.at[96:128], xs.at[0, 0:32], row_dev(1))]
    up0 = send(lat.at[0:64], xs.at[3, 32:96], dev(dz=1))
    dn1 = send(lat.at[64:128], xs.at[1, 96:160], dev(dz=-1))
    up1 = send(lat.at[64:128], xs.at[3, 96:160], dev(dz=1))
    dn0 = send(lat.at[0:64], xs.at[1, 32:96], dev(dz=-1))
    part = {0: send(lat, xs.at[4, 32:160], dev(flip=True))}

    lane = lax.broadcasted_iota(jnp.int32, (640, 128), 1)
    chan = lax.broadcasted_iota(jnp.int32, (640, 128), 0)
    place = lane + 10 * ((lane * 205) >> 11)
    for s in range(8):
        core = k if s < 4 else 1 - k
        hit = (chan == place + (zh + s % 4) % 4 * 160 + core * 10) & (lane < 80)
        st[:, s * 128 : s * 128 + 128] = jnp.where(hit, 1.0, 0.0).astype(BF16)

    l0 = lax.broadcasted_iota(jnp.int32, (128, 768), 0)
    q = lax.broadcasted_iota(jnp.int32, (128, 768), 1)
    tap = (l0 * 205) >> 11
    third = (tap * 11) >> 5
    want = third * 256 + (tap - 3 * third) * 80 + l0 - 10 * tap
    diff = jnp.where(l0 < 90, q - want, -1)
    for j, dy in enumerate(BLOCKS):
        hit = jnp.where(diff == (y + dy) % 8 * 10, 1.0, 0.0)
        sk[j * 128 : j * 128 + 128, :] = hit.astype(BF16)

    loads[2].wait()
    ts[...] = dot(st[...], tgt[...], (((0,), (1,)), ((), ()))).astype(BF16)
    tb[0] = ts[0:80]
    right, left, fwd_r, fwd_l = {}, {}, {}, {}

    halo = {0: (top[0], bot[0])}

    def halos(s):
        up = send(xs.at[s, 32:64], xs.at[s, 160:192], row_dev(-1))
        dn = send(xs.at[s, 128:160], xs.at[s, 0:32], row_dev(1))
        halo[s] = (up, dn)
        part[s] = send(xs.at[s, 32:160], xs.at[s + 4, 32:160], dev(flip=True))

    def x_sends(dy):
        got = kp.at[0, :, :, blk(-dy)]
        right[dy] = send(got, kp.at[3, :, :, blk(-dy)], dev(dx=1))
        left[dy] = send(got, kp.at[1, :, :, blk(-dy)], dev(dx=-1))

    def y_near(dy):
        p1[dy, 1].recv()
        p1[dy, 0].recv()
        if dy in (2, -2):
            one, half = dy // 2, 0 if dy > 0 else 1
            dst = kp.at[0, half, :, blk(4)]
            late[half] = send(kp.at[0, half, :, blk(-dy)], dst, dev(dy=dy))
            got = kp.at[0, :, :, blk(-dy)]
            late[dy + one] = send(got, kp.at[0, :, :, blk(-dy - one)], dev(dy=one))
        x_sends(dy)

    ends = {}

    def edges(s):
        ends[s] = []
        for c, edge in zip(halo[s], (slice(160, 192), slice(0, 32))):
            c.recv()
            ends[s].append(send(xs.at[s, edge], xs.at[s + 4, edge], dev(flip=True)))

    def x_step(dy):
        right[dy].recv()
        dst = kp.at[2, 0, :, blk(-dy)]
        fwd_r[dy] = send(kp.at[3, 0, :, blk(-dy)], dst, dev(dx=1))
        left[dy].recv()
        dst = kp.at[2, 1, :, blk(-dy)]
        fwd_l[dy] = send(kp.at[1, 1, :, blk(-dy)], dst, dev(dx=-1))

    def to_group(src_of, dst_of, hops):
        sent = {}
        for s in (4, 1, 3, 5, 7):
            back = s // 4 * 4 + (-s) % 4
            sent[back] = send(src_of(s), dst_of(back), dev(dz=s % 4, flip=s >= 4))
        up = send(src_of(2), hops.at[0], dev(dz=1))
        dn = send(src_of(6), hops.at[1], dev(dz=-1))

        def relay_up():
            up.recv()
            sent[2] = send(hops.at[0], dst_of(2), dev(dz=1))

        def relay_dn():
            dn.recv()
            sent[6] = send(hops.at[1], dst_of(6), dev(dz=-1, flip=True))

        return sent, relay_up, relay_dn

    p1[0, 1].recv()
    x_sends(0)
    y_near(2)
    y_near(-2)
    y_near(1)
    y_near(-1)
    x_step(0)
    up0.recv()
    over0 = send(xs.at[3, 32:96], xs.at[2, 32:96], dev(dz=1))
    dn1.recv()
    over1 = send(xs.at[1, 96:160], xs.at[2, 96:160], dev(dz=-1))
    x_step(2)
    x_step(-2)
    for dy in (3, -3):
        late[dy].recv()
        x_sends(dy)
    late[0].recv()
    late[1].recv()
    x_sends(4)
    x_step(1)
    x_step(-1)
    up1.recv()
    halos(3)
    dn0.recv()
    halos(1)
    goals, goal_up, goal_dn = to_group(
        lambda s: ts.at[s * 128 : s * 128 + 80], lambda s: tb.at[s], tr
    )
    x_step(3)
    x_step(-3)
    over0.recv()
    over1.recv()
    halos(2)
    x_step(4)
    edges(0)
    edges(3)
    edges(1)

    def place_kernel(dx):
        out = dot(kp[dx].reshape(160, 1024), sk[...]).astype(BF16)
        km[rows_of(dx, 0), :] = out[:80]
        km[rows_of(dx, 1), :] = out[80:]

    place_kernel(0)
    edges(2)
    goal_up()
    goal_dn()
    place_kernel(1)
    place_kernel(3)

    for dy in range(8):
        dy = dy if dy < 5 else dy - 8
        fwd_r[dy].recv()
        fwd_l[dy].recv()
    place_kernel(2)

    col = lax.broadcasted_iota(jnp.int32, (256, 128), 0) % 32
    first, last = col == 0, col == 31
    real = lax.broadcasted_iota(jnp.int32, (256, 128), 1) < 80

    def pair_ready(s):
        part[s].recv()
        for c in ends[s]:
            c.recv()
            c.sent()

        @pl.when(row == 0)
        def _():
            xs[s, 0:32, :] = jnp.zeros((32, 640), BF16)
            xs[s + 4, 0:32, :] = jnp.zeros((32, 640), BF16)

        @pl.when(row == 7)
        def _():
            xs[s, 160:192, :] = jnp.zeros((32, 640), BF16)
            xs[s + 4, 160:192, :] = jnp.zeros((32, 640), BF16)

        for back in (s, s + 4):
            if back:
                goals[back].recv()

    def joined(ref, s, rows):
        return jnp.concatenate([ref[s, rows], ref[s + 4, rows]], axis=0)

    def widened(err):
        zero = jnp.zeros((256, 128), F32)
        nxt = jnp.where(last, 0.0, pltpu.roll(err, 255, 0))
        prv = jnp.where(first, 0.0, pltpu.roll(err, 1, 0))
        wide = jnp.concatenate([nxt, zero], axis=1)
        wide = wide + pltpu.roll(jnp.concatenate([err, zero], axis=1), 80, 1)
        wide = wide + pltpu.roll(jnp.concatenate([prv, zero], axis=1), 160, 1)
        return wide.astype(BF16)

    def forward(s):
        acc = None
        for a in range(3):
            win = joined(xs, s, slice(32 * a, 32 * a + 128))
            term = dot(win, km[:, 256 * a : 256 * a + 256])
            acc = term if acc is None else acc + term
        mid = pltpu.roll(acc, 176, 1)[:, :128]
        end = pltpu.roll(acc, 96, 1)[:, :128]
        total = mid + jnp.where(first, 0.0, pltpu.roll(acc[:, :128], 1, 0))
        total = total + jnp.where(last, 0.0, pltpu.roll(end, 255, 0))
        stu = jnp.where(real, total, 0.0).astype(BF16)
        stu = stu.astype(F32)
        goal = []
        for i, at in enumerate((s, s + 4)):
            sn[at] = stu[128 * i : 128 * i + 128].astype(BF16)
            fill = jnp.zeros((48, 128), F32)
            goal.append(jnp.concatenate([tb[at].astype(F32), fill], axis=0).T)
        err = stu - jnp.concatenate(goal, axis=0)
        err = err.astype(BF16).astype(F32)
        for i, at in enumerate((s, s + 4)):
            eb[at] = err[128 * i : 128 * i + 128].astype(BF16)
        wide = widened(err)
        e3[s, 32:160, :] = wide[:128]
        e3[s + 4, 32:160, :] = wide[128:]

    err_halos = []
    for s in (0, 3, 1, 2):
        pair_ready(s)
        forward(s)
    err_halos.append(send(eb.at[:, 0:32], hb.at[1], row_dev(-1)))
    err_halos.append(send(eb.at[:, 96:128], hb.at[0], row_dev(1)))
    gacc[...] = jnp.zeros((640, 768), F32)

    def weight_grad(m, carry):
        two = pl.ds(2 * m, 2)
        errs = e3[two, 32:160, :].reshape(256, 256)
        for a in range(3):
            win = xs[two, 32 * a : 32 * a + 128, :].reshape(256, 640)
            gacc[:, 256 * a : 256 * a + 256] += dot(win, errs, TN)
        return carry

    lax.fori_loop(0, 4, weight_grad, 0)
    gb[...] = gacc[...].astype(BF16)

    first_hop, raw, second_hop = [], [], []

    def place_grad(g):
        cols = slice(*GROUPS[g])
        ga[:, cols] = dot(gb[...], sk[cols, :], NT).astype(BF16)
        up = send(ga.at[rows_of(2, 0), cols], ra.at[0, :, cols], dev(dx=1))
        dn = send(ga.at[rows_of(2, 1), cols], ra.at[1, :, cols], dev(dx=-1))
        first_hop.append((up, dn))
        up = send(ga.at[rows_of(1, 1), cols], rd.at[1, :, cols], dev(dx=1))
        dn = send(ga.at[rows_of(3, 0), cols], rd.at[0, :, cols], dev(dx=-1))
        raw.append((up, dn))

    def relay(g):
        cols = slice(*GROUPS[g])
        up, dn = first_hop[g]
        up.recv()
        rs[0, :, cols] = (ra[0, :, cols].astype(F32) + ga[rows_of(1, 0), cols].astype(F32)).astype(BF16)
        up = send(rs.at[0, :, cols], rd.at[2, :, cols], dev(dx=1))
        dn.recv()
        rs[1, :, cols] = (ra[1, :, cols].astype(F32) + ga[rows_of(3, 1), cols].astype(F32)).astype(BF16)
        dn = send(rs.at[1, :, cols], rd.at[3, :, cols], dev(dx=-1))
        second_hop.append((up, dn))

    ysent = []

    def spread(g):
        cols = slice(*GROUPS[g])
        for c in raw[g] + second_hop[g]:
            c.recv()
        for i in range(2):
            mine = ga[rows_of(0, i), cols].astype(F32)
            both = rd[i, :, cols].astype(F32) + rd[i + 2, :, cols].astype(F32)
            ysend[i, :, cols] = (mine + both).astype(BF16)
        for dy in BLOCKS[cols.start // 128 : cols.stop // 128]:
            if dy:
                ysent.append(send(ysend.at[:, :, blk(dy)], yr.at[len(ysent)], dev(dy=dy)))

    place_grad(0)
    place_grad(1)
    place_grad(2)
    for s in range(8):
        sb[s] = sn[s].astype(F32).T[:80].astype(BF16)
    stus, stu_up, stu_dn = to_group(
        lambda s: sb.at[s], lambda s: rb.at[s * 128 : s * 128 + 80], sr
    )
    rb[0:80] = sb[0]
    for c in err_halos:
        c.recv()
    for i, edge in enumerate((slice(0, 32), slice(160, 192))):
        wide = widened(hb[i].reshape(256, 128).astype(F32))
        e3[:, edge, :] = wide.reshape(8, 32, 256)

    @pl.when(row == 0)
    def _():
        e3[:, 0:32, :] = jnp.zeros((8, 32, 256), BF16)

    @pl.when(row == 7)
    def _():
        e3[:, 160:192, :] = jnp.zeros((8, 32, 256), BF16)

    ip = {}

    def input_grad(s):
        acc = None
        for a in range(3):
            win = e3[s : s + 2, 64 - 32 * a : 192 - 32 * a, :].reshape(256, 256)
            term = dot(win, km[:, 256 * a : 256 * a + 256], NT)
            acc = term if acc is None else acc + term
        igp[s : s + 2] = acc.astype(BF16).reshape(2, 128, 640)
        if s >= 4:
            ip[s - 4] = send(igp.at[s : s + 2], igr.at[s - 4 : s - 2], dev(flip=True))

    def core_sum(s):
        igc[s] = (igp[s].astype(F32) + igr[s].astype(F32)).astype(BF16)

    input_grad(6)
    input_grad(2)
    ip[2].recv()
    core_sum(2)
    ir_a = send(igc.at[2, 0:64], ia.at[0], dev(dz=1))
    ir_b = send(igc.at[2, 64:128], ia.at[1], dev(dz=-1))
    core_sum(3)
    id_b = send(igc.at[3, 0:64], idr.at[0], dev(dz=-1))
    stu_up()
    stu_dn()
    input_grad(4)
    relay(0)
    input_grad(0)
    ip[0].recv()
    core_sum(1)
    id_a = send(igc.at[1, 64:128], idr.at[1], dev(dz=1))
    core_sum(0)
    relay(1)
    relay(2)
    spread(0)
    spread(1)

    ir_a.recv()
    isum[0] = (ia[0].astype(F32) + igc[1, 0:64].astype(F32)).astype(BF16)
    is_a = send(isum.at[0], idr.at[2], dev(dz=1))
    ir_b.recv()
    isum[1] = (ia[1].astype(F32) + igc[3, 64:128].astype(F32)).astype(BF16)
    is_b = send(isum.at[1], idr.at[3], dev(dz=-1))

    spread(2)
    total = ysend[:, :, blk(0)].astype(F32)
    for i in range(7):
        ysent[i].recv()
        total = total + yr[i].astype(F32)
    zs[...] = total
    zc = send(zs.at[1], zr, dev(flip_zl=True))
    for c in stus.values():
        c.recv()
    stu_out[...] = dot(rb[...], st[...], (((0,), (1,)), ((), ()))).astype(BF16)


    for c in (id_a, id_b, is_a, is_b):
        c.recv()
    low = igc[0, 0:64].astype(F32) + idr[0].astype(F32) + idr[2].astype(F32)
    high = igc[0, 64:128].astype(F32) + idr[1].astype(F32) + idr[3].astype(F32)
    ig_out[0:64] = low.astype(BF16)
    ig_out[64:128] = high.astype(BF16)

    zc.recv()
    total = zs[0] + zr[...]
    grad = total * (1.0 / 64.0)
    turned = jnp.concatenate([grad, jnp.zeros((48, 128), F32)], axis=0).T
    for t in range(9):
        g_out[t] = turned[10 * t : 10 * t + 10, :80]
    for c in copies:
        c.sent()


def per_device(latents, target, weight, moment1, moment2):
    vmem = pl.BlockSpec(memory_space=pltpu.VMEM)
    student, input_grad, grad = pl.pallas_call(
        kernel,
        out_shape=(
            jax.ShapeDtypeStruct((128, 640), BF16),
            jax.ShapeDtypeStruct((128, 640), BF16),
            jax.ShapeDtypeStruct((9, 10, 80), F32),
        ),
        in_specs=[pl.BlockSpec(memory_space=pl.ANY)] * 3,
        out_specs=(vmem,) * 3,
        scratch_shapes=[
            pltpu.VMEM((4, 2, 80, 1024), BF16),
            pltpu.VMEM((640, 768), BF16),
            pltpu.VMEM((8, 192, 640), BF16),
            pltpu.VMEM((640, 1024), BF16),
            pltpu.VMEM((1024, 768), BF16),
            pltpu.VMEM((1024, 128), BF16),
            pltpu.VMEM((8, 80, 128), BF16),
            pltpu.VMEM((2, 80, 128), BF16),
            pltpu.VMEM((8, 128, 128), BF16),
            pltpu.VMEM((8, 80, 128), BF16),
            pltpu.VMEM((2, 80, 128), BF16),
            pltpu.VMEM((1024, 128), BF16),
            pltpu.VMEM((8, 128, 128), BF16),
            pltpu.VMEM((2, 8, 32, 128), BF16),
            pltpu.VMEM((8, 192, 256), BF16),
            pltpu.VMEM((640, 768), F32),
            pltpu.VMEM((640, 768), BF16),
            pltpu.VMEM((640, 1024), BF16),
            pltpu.VMEM((2, 80, 1024), BF16),
            pltpu.VMEM((2, 80, 1024), BF16),
            pltpu.VMEM((4, 80, 1024), BF16),
            pltpu.VMEM((2, 80, 1024), BF16),
            pltpu.VMEM((7, 2, 80, 128), BF16),
            pltpu.VMEM((2, 80, 128), F32),
            pltpu.VMEM((80, 128), F32),
            pltpu.VMEM((8, 128, 640), BF16),
            pltpu.VMEM((4, 128, 640), BF16),
            pltpu.VMEM((4, 128, 640), BF16),
            pltpu.VMEM((2, 64, 640), BF16),
            pltpu.VMEM((2, 64, 640), BF16),
            pltpu.VMEM((4, 64, 640), BF16),
            pltpu.VMEM((128, 640), BF16),
            pltpu.VMEM((9, 10, 80), F32),
            pltpu.SemaphoreType.DMA((3,)),
            pltpu.SemaphoreType.DMA((N_SEM,)),
            pltpu.SemaphoreType.DMA((N_SEM,)),
        ],
        compiler_params=pltpu.CompilerParams(
            collective_id=0, has_side_effects=True, vmem_limit_bytes=48 << 20
        ),
    )(latents.reshape(128, 640), target.reshape(128, 640), weight.transpose(0, 2, 1))
    grad = grad.transpose(0, 2, 1)
    new_moment1 = 0.9 * moment1 + 0.1 * grad
    new_moment2 = 0.999 * moment2 + 0.001 * grad * grad
    new_weight = weight - 0.01 * new_moment1 / (jnp.sqrt(new_moment2) + 1e-08)
    return (
        student.reshape(latents.shape),
        input_grad.reshape(latents.shape),
        new_weight,
        new_moment1,
        new_moment2,
    )


def solution(mesh):
    act = P("dp", "rows", None, None)
    par = P(None, "rows", "dp")
    return jax.shard_map(
        per_device,
        mesh=mesh,
        in_specs=(act, act, par, par, par),
        out_specs=(act, act, par, par, par),
        check_vma=False,
    )
```
